128 devices in a mesh: gx: 16 (over z, x), gy: 8 (over y, core).
Axes of the slice: x: 4, y: 4, z: 4, core: 2. Of those that a mesh axis runs over, the one named last changes fastest.
Arguments:
- positions: float32 [3, 262144], P(None, ('gx', 'gy')), may hold values from -6 to 6
- velocities: float32 [3, 262144], P(None, ('gx', 'gy')), may hold values from -6 to 6
- masses: float32 [262144], P(('gx', 'gy')), may hold values from 0.25 to 4
- labels: int32 [262144, 1], P(('gx', 'gy')), may hold values from 0 to 1023; in each aligned block of 2048 rows (0 to 2047, 2048 to 4095, ...) at most 4 rows name the same one
- owner_slot: int32 [1024], replicated, may hold values from 0 to 1023, each once
- group_cap: int32 [1024], replicated, may hold values from 512 to 4095
Outputs:
- compact_index: int32 [262144], P(('gx', 'gy'))
- potential: float32 [262144], P(('gx', 'gy'))
- binding: float32 [262144], P(('gx', 'gy'))
- catalog: float32 [4, 1024], P(None, ('gx', 'gy'))
The draws below stay inside these ranges and needn't reach their ends.
Inputs may be any that keep to these rules, and one draw needn't show every extreme that they name: `labels`: on each device's 2048 particles no label occurs more than 4 times; some label occurs exactly 4 times in some devices' particles; every label occurs somewhere. `owner_slot` is a permutation. Group g is owned by device owner_slot[g] // 8 (devices numbered along gx then gy) as its local group owner_slot[g] % 8.
All inputs are finite; a program needn't handle non-finite values.
Results may differ from the reference program's by a relative error of at most 0.0003.
Values sent between devices are 32-bit elements; how exact they have to be, the bound alone decides.
A program may use at most 64 MiB of HBM per device.

```python
import math
import jax
import jax.numpy as jnp
import numpy as np
from jax import lax

P_SIZE = 2048
CAP = 2048
G = 1024
MOST = 4
N = 262144


def touch_ends(drawn, rng, low, largest):
    dims = drawn.shape
    place = [jax.random.randint(jax.random.fold_in(rng, axis), (), 0, dims[axis]) for axis in range(len(dims))]
    drawn = drawn.at[tuple(place)].set(low)
    longest = dims.index(max(dims))
    place[longest] = (place[longest] + 1) % dims[longest]
    return drawn.at[tuple(place)].set(largest)


def block_levels(rng, extent, split, smallest, high):
    def one(axis_at, shards_of):
        steps = jax.random.uniform(jax.random.fold_in(jax.random.fold_in(rng, 6), axis_at), (shards_of,), jnp.float32, smallest / len(split), high / len(split))
        return jnp.repeat(jnp.exp(steps), extent[axis_at] // shards_of).reshape((-1,) + (1,) * (len(extent) - axis_at - 1))

    gain = one(*split[0])
    for cut in split[1:]:
        gain = gain * one(*cut)
    return gain


def shared_out(key, own, number, rows, amount, top, most, skew):
    order = jax.random.permutation(key, amount)
    crowded, usual = portions_of(amount, rows * top, most, skew, True), portions_of(amount, rows * top, most, skew, False)
    places = jnp.arange(amount)

    def named(tallies, offset_by):
        used = int((tallies > 0).sum())
        fixed = max(1, used // 4)
        moved = fixed + (places - fixed + offset_by * (used - fixed)) % max(1, amount - fixed)
        return jnp.zeros((amount,), jnp.int32).at[order[jnp.where(places < fixed, places, moved)]].set(jnp.asarray(tallies, jnp.int32))

    tallies = jnp.where(number % 4 == 0, named(crowded, number // 4), named(usual, number - number // 4 - 1))
    mixed = jax.random.permutation(jax.random.fold_in(own, 3), amount)
    source_of, taker = mixed[0:amount // 2 * 2:2], mixed[1:amount // 2 * 2:2]
    room = jnp.minimum(tallies[source_of] - 1, most - tallies[taker]) // 2
    room = jnp.where((source_of == order[0]) | (taker == order[0]) | (tallies[taker] == 0), 0, jnp.maximum(room, 0))
    moved = jax.random.randint(jax.random.fold_in(own, 4), (amount // 2,), 0, 1 << 20) % (room + 1)
    tallies = tallies.at[source_of].add(-moved).at[taker].add(moved)
    members = jnp.searchsorted(jnp.cumsum(tallies), jnp.arange(rows * top), side="right").astype(jnp.int32)
    grid = members.reshape(top, rows).T
    grid = grid[jax.random.permutation(jax.random.fold_in(own, 1), rows)]
    offset_by = jax.random.randint(jax.random.fold_in(own, 2), (rows, 1), 0, top)
    return jnp.take_along_axis(grid, (jnp.arange(top)[None, :] + offset_by) % top, axis=1)


def portions_of(number_of, total, reach, slope, full):
    weights = [(1 << 20) // math.isqrt(grade ** slope) + 1 for grade in range(1, number_of + 1)]
    largest = reach if full else min(reach, max(-(-total // number_of), total * weights[0] // sum(weights)))
    least = 1 if total - largest >= number_of - 1 else 0
    counts, spare = [largest] + [least] * (number_of - 1), total - largest - least * (number_of - 1)
    while spare > 0:
        movable = [i for i in range(1, number_of) if counts[i] < largest] or [i for i in range(1, number_of) if counts[i] < reach]
        pool, left = sum([weights[i] for i in movable]), spare
        for i in movable:
            extra = min(reach - counts[i], max(1, left * weights[i] // pool), spare)
            counts[i] = counts[i] + extra
            spare = spare - extra
    return np.array(counts)


def noise(rng, shape, spread, limit, cuts=(), kind=jnp.bfloat16):
    factor_of = block_levels(rng, shape, cuts, -0.22, 0.18) if cuts else 1.0
    result = jax.random.normal(rng, shape, jnp.float32) * spread * factor_of
    return jnp.minimum(jnp.maximum(result, -limit), limit).astype(kind)


def setup_inputs(seed: int = 0) -> dict:
    keys = jax.random.split(jax.random.key(seed), 7)
    positions = noise(keys[0], (3, N), 1.0, 6.0, ((1, 128),), jnp.float32)
    velocities = noise(keys[1], (3, N), 1.0, 6.0, ((1, 128),), jnp.float32)
    masses = jnp.clip(jnp.exp(math.log(4.0) - 2.7725887 * jax.random.uniform(keys[2], (N,), jnp.float32) ** block_levels(keys[2], (N,), ((0, 128),), -0.2, 0.2)), 0.25, 4.0)
    labels_keys = jax.random.split(jax.random.fold_in(keys[3], 1), N // P_SIZE)
    labels_turns = jax.random.permutation(jax.random.fold_in(keys[3], 3), N // P_SIZE)
    labels = jax.vmap(lambda own, number: shared_out(jax.random.fold_in(keys[3], 2), own, number, P_SIZE, G, 1, MOST, 3))(labels_keys, labels_turns).reshape((N, 1))
    owner_slot = jax.random.permutation(keys[4], G).astype(jnp.int32)
    group_cap = touch_ends(jax.random.randint(keys[5], (G,), CAP // 4, 2 * CAP), jax.random.fold_in(keys[5], 1), CAP // 4, (2 * CAP) - 1).astype(jnp.int32)
    return dict(positions=positions, velocities=velocities, masses=masses, labels=labels, owner_slot=owner_slot, group_cap=group_cap)


softening_sq = 0.0025

def group_potential(block):
    coords = block[0:3]
    weights = block[6]
    width = min(512, CAP)
    column_ids = jnp.arange(CAP, dtype=jnp.int32)

    def row_part(row_start):
        near = lax.dynamic_slice_in_dim(coords, row_start, width, 1)
        row_ids = row_start + jnp.arange(width, dtype=jnp.int32)
        dist_sq = lax.optimization_barrier(jnp.sum((near[:, :, None] - coords[:, None, :]) ** 2, axis=0))
        inverse = jnp.where(row_ids[:, None] == column_ids[None, :], 0.0, lax.rsqrt(dist_sq + softening_sq))
        return -lax.optimization_barrier(jnp.sum(inverse * weights[None, :], axis=1)) / CAP
    starts = jnp.arange(CAP // width, dtype=jnp.int32) * width
    return lax.map(row_part, starts).reshape(CAP)

def reference(positions, velocities, masses, labels, owner_slot, group_cap):
    label_flat = labels[:, 0]
    count_all = label_flat.shape[0]
    ngroups = owner_slot.shape[0]
    order = jnp.argsort(label_flat, stable=True).astype(jnp.int32)
    totals = jax.ops.segment_sum(jnp.ones_like(label_flat), label_flat, ngroups).astype(jnp.int32)
    firsts = jnp.cumsum(totals).astype(jnp.int32) - totals
    sorted_labels = label_flat[order]
    ranks = jnp.zeros_like(label_flat).at[order].set(jnp.arange(count_all, dtype=jnp.int32) - firsts[sorted_labels])
    limits = jnp.minimum(group_cap, CAP)
    kept_counts = jnp.minimum(totals, limits)
    starts = jnp.cumsum(kept_counts).astype(jnp.int32) - kept_counts
    keep = ranks < limits[label_flat]
    compact_index = jnp.where(keep, starts[label_flat] + ranks, -1).astype(jnp.int32)
    slot = jnp.where(keep, label_flat * CAP + ranks, ngroups * CAP).astype(jnp.int32)
    fields = jnp.concatenate([positions, velocities, masses[None, :]], axis=0)
    compact = jnp.zeros((7, ngroups * CAP), jnp.float32).at[:, slot].set(fields, mode='drop')
    compact = jnp.transpose(compact.reshape(7, ngroups, CAP), (1, 0, 2))
    pot = lax.map(group_potential, compact)
    weights = compact[:, 6, :]
    mass_sum = lax.optimization_barrier(jnp.sum(weights, axis=1))
    bulk = lax.optimization_barrier(jnp.sum(weights[:, None, :] * compact[:, 3:6, :], axis=2)) / mass_sum[:, None]
    energy = 0.5 * lax.optimization_barrier(jnp.sum((compact[:, 3:6, :] - bulk[:, :, None]) ** 2, axis=1)) + pot
    safe = jnp.minimum(slot, ngroups * CAP - 1)
    potential = jnp.where(keep, pot.reshape(-1)[safe], 0.0)
    binding = jnp.where(keep, energy.reshape(-1)[safe], 0.0)
    stats = jnp.concatenate([mass_sum[None, :] / CAP, jnp.transpose(bulk)], axis=0)
    catalog = jnp.zeros((4, ngroups), jnp.float32).at[:, owner_slot].set(stats)
    return (compact_index, potential, binding, catalog)
```

```python
import functools

import jax
import jax.numpy as jnp
from jax import lax
from jax.experimental import pallas as pl
from jax.experimental.pallas import tpu as pltpu
from jax.sharding import PartitionSpec as P

CAP = 2048
SOFTENING_SQ = 0.0025
MOST = 4
LANES = 128
MESH = pl.DeviceIdType.MESH
F32, BF16, I32 = jnp.float32, jnp.bfloat16, jnp.int32


def iota(shape, axis):
    return lax.broadcasted_iota(I32, shape, axis)


def onehot(index_row, depth):
    hit = iota((depth, index_row.shape[1]), 0) == index_row
    return jnp.where(hit, 1.0, 0.0).astype(BF16)


def parts_of(value, count):
    found = []
    for step in range(count):
        part = value.astype(BF16)
        found.append(part)
        if step < count - 1:
            value = value - part.astype(F32)
    return found


def dot(left, right):
    return lax.dot_general(left, right, (((1,), (0,)), ((), ())), preferred_element_type=F32)


def dot_nt(left, right):
    return lax.dot_general(left, right, (((1,), (1,)), ((), ())), preferred_element_type=F32)


def quad_sum(value):
    rows = value.shape[0]
    row = iota(value.shape, 0)
    for step in (1, 2):
        up = pltpu.roll(value, rows - step, 0)
        down = pltpu.roll(value, step, 0)
        value = value + jnp.where((row & step) == 0, up, down)
    return value


def exchange(here, out, mid, got, sends, recvs, local_sem, sizes):
    mx, my = here
    nx, ny = sizes
    own = pltpu.make_async_copy(
        out.at[:, pl.ds(my, 1), :], mid.at[:, pl.ds(my, 1), :], local_sem.at[0]
    )
    own.start()
    copies = []
    for step in range(1, ny):
        peer = lax.rem(my + step, ny)
        copy = pltpu.make_async_remote_copy(
            src_ref=out.at[:, pl.ds(peer, 1), :],
            dst_ref=mid.at[:, pl.ds(my, 1), :],
            send_sem=sends.at[step],
            recv_sem=recvs.at[step],
            device_id=(mx, peer),
            device_id_type=MESH,
        )
        copy.start()
        copies.append(copy)
    own.wait()
    for copy in copies:
        copy.wait()
    own = pltpu.make_async_copy(mid.at[mx], got.at[mx], local_sem.at[1])
    own.start()
    copies = []
    for step in range(1, nx):
        peer = lax.rem(mx + step, nx)
        copy = pltpu.make_async_remote_copy(
            src_ref=mid.at[peer],
            dst_ref=got.at[mx],
            send_sem=sends.at[ny + step],
            recv_sem=recvs.at[ny + step],
            device_id=(peer, my),
            device_id_type=MESH,
        )
        copy.start()
        copies.append(copy)
    own.wait()
    for copy in copies:
        copy.wait()


def kernel(
    sizes, lab_ref, lab16_ref, pos_ref, vel_ref, mass_ref, slot8_ref, slot_ref, cap_ref,
    index_ref, pot_ref, bind_ref, cat_ref,
    out1, mid1, got1, out2, mid2, got2, hot_label, hot_dest, hot_group, near, total,
    send1, recv1, send2, recv2, local_sem,
):
    nx, ny = sizes
    devices = nx * ny
    mx, my = lax.axis_index("gx"), lax.axis_index("gy")
    me = mx * ny + my
    count = lab_ref.shape[1]
    groups = slot_ref.shape[1]
    owned = groups // devices
    slots = owned * MOST
    blocks = count // LANES

    barrier = pltpu.get_barrier_semaphore()
    for step in range(1, ny):
        pl.semaphore_signal(barrier, inc=1, device_id=(mx, lax.rem(my + step, ny)), device_id_type=MESH)
    for step in range(1, nx):
        pl.semaphore_signal(barrier, inc=1, device_id=(lax.rem(mx + step, nx), my), device_id_type=MESH)

    label = lab_ref[...]
    label_high, label_low = label >> 7, label & 127
    hot_label[...] = onehot(label_low, LANES)
    slot8 = slot8_ref[...]
    table = jnp.concatenate([slot8 // owned, slot8 % owned], axis=0).astype(F32).astype(BF16)
    found = dot(table, hot_label[...])
    high_hit = iota((groups // LANES, count), 0) == label_high
    half = groups // LANES
    dest = jnp.sum(jnp.where(high_hit, found[:half], 0.0), axis=0, keepdims=True).astype(I32)
    local_group = jnp.sum(jnp.where(high_hit, found[half:], 0.0), axis=0, keepdims=True).astype(I32)

    columns = jnp.concatenate(
        [lab16_ref[...], jnp.zeros((LANES - blocks, LANES), I32)], axis=0
    ).astype(F32).T.astype(I32)
    ranks = []
    triangle = iota((LANES, LANES), 0) < iota((LANES, LANES), 1)
    for block in range(blocks):
        mine = label[:, block * LANES : (block + 1) * LANES]
        ranks.append(jnp.zeros((8, LANES), I32))
    for other in range(blocks):
        column = jnp.broadcast_to(columns[:, other : other + 1], (LANES, LANES))
        for block in range(other, blocks):
            mine = label[:, block * LANES : (block + 1) * LANES]
            same = column == mine
            if block == other:
                same = same & triangle
            hits = jnp.where(same, 1, 0)
            ranks[block] = ranks[block] + jnp.sum(hits.reshape(LANES // 8, 8, LANES), axis=0)
    rank = jnp.concatenate([jnp.sum(r, axis=0, keepdims=True) for r in ranks], axis=1)
    slot = local_group * MOST + rank

    hot_dest[...] = onehot(dest, devices)
    slot_hit = iota((slots, count), 0) == slot
    fields = [pos_ref[0:1, :], pos_ref[1:2, :], pos_ref[2:3, :], mass_ref[...],
              vel_ref[0:1, :], vel_ref[1:2, :], vel_ref[2:3, :]]
    split = [[part.astype(F32) for part in parts_of(field, 3)] for field in fields]
    for half_row in range(2):
        rows = None
        for part in range(3):
            chosen = [
                jnp.where(slot_hit, split[f][part], 0.0).astype(BF16)
                for f in range(half_row * 4, min(half_row * 4 + 4, 7))
            ]
            if half_row == 1:
                chosen.append(jnp.zeros((slots, count), BF16))
            product = dot_nt(hot_dest[...], jnp.concatenate(chosen, axis=0))
            rows = product if rows is None else rows + product
        out1[:, :, half_row * LANES : (half_row + 1) * LANES] = rows.reshape(nx, ny, LANES)

    slot_row = slot_ref[...]
    hot_group[...] = onehot(slot_row // owned, devices)
    row32 = iota((slots, 1), 0)
    limits = jnp.minimum(cap_ref[...], CAP).astype(F32)
    limit = jnp.sum(
        jnp.where(slot_row == me * owned + row32 // MOST, limits, 0.0), axis=1, keepdims=True
    )
    upper = jnp.where(iota((LANES, LANES), 0) < iota((LANES, LANES), 1), 1.0, 0.0).astype(BF16)

    pl.semaphore_wait(barrier, nx + ny - 2)
    exchange((mx, my), out1, mid1, got1, send1, recv1, local_sem.at[0], sizes)

    first = got1[:, :, :LANES].reshape(devices, LANES)
    second = got1[:, :, LANES:].reshape(devices, LANES)
    first_t, second_t = first.T, second.T
    mass_t = first_t[3 * slots :]
    valid = mass_t > 0.0
    tally = quad_sum(jnp.where(valid, 1.0, 0.0))
    before = dot(tally.astype(BF16), upper)
    member_rank = before + (row32 % MOST).astype(F32)
    keep = valid & (member_rank < limit)
    kept_mass = jnp.where(keep, mass_t, 0.0)
    kept_total = quad_sum(jnp.sum(jnp.where(keep, 1.0, 0.0), axis=1, keepdims=True))
    near[0 : LANES] = jnp.concatenate([first[:, : 3 * slots], jnp.concatenate(
        [kept_mass, jnp.zeros((LANES - slots, LANES), F32)], axis=0).T[:, :slots]], axis=1)
    near[LANES :] = first_t
    total[...] = jnp.zeros_like(total)
    offset = iota((8, LANES), 1) - iota((8, LANES), 0)

    def rows_of(step, carry):
        source = near[pl.ds(pl.multiple_of(step * 8, 8), 8), :]
        diagonal = offset == step * 8
        for group in range(owned):
            base = group * MOST
            here = [
                [jnp.broadcast_to(near[LANES + f * slots + base + r : LANES + f * slots + base + r + 1, :], (8, LANES)) for f in range(3)]
                for r in range(MOST)
            ]
            sums = [total[base + r] for r in range(MOST)]
            for other in range(MOST):
                there = [
                    jnp.broadcast_to(source[:, f * slots + base + other : f * slots + base + other + 1], (8, LANES))
                    for f in range(4)
                ]
                for r in range(MOST):
                    dx = here[r][0] - there[0]
                    dy = here[r][1] - there[1]
                    dz = here[r][2] - there[2]
                    inverse = lax.rsqrt(dx * dx + dy * dy + dz * dz + SOFTENING_SQ)
                    if r == other:
                        inverse = jnp.where(diagonal, 0.0, inverse)
                    sums[r] = sums[r] + inverse * there[3]
            for r in range(MOST):
                total[base + r] = sums[r]
        return carry

    lax.fori_loop(0, devices // 8, rows_of, 0)
    pot = jnp.sum(total[...], axis=1) * (-1.0 / CAP)

    mass_sum = quad_sum(jnp.sum(kept_mass, axis=1, keepdims=True))
    energy = None
    stats = [mass_sum * (1.0 / CAP)]
    for axis in range(3):
        speed = second_t[axis * slots : (axis + 1) * slots]
        bulk = quad_sum(jnp.sum(kept_mass * speed, axis=1, keepdims=True)) / mass_sum
        stats.append(bulk)
        apart = (speed - bulk) * (speed - bulk)
        energy = apart if energy is None else energy + apart
    energy = 0.5 * energy + pot
    pick = iota((slots, owned), 0) == iota((slots, owned), 1) * MOST
    for number, stat in enumerate(stats):
        cat_ref[number : number + 1, :] = jnp.sum(jnp.where(pick, stat, 0.0), axis=0, keepdims=True)
    reply = jnp.concatenate(
        [pot, energy, jnp.where(keep, member_rank, -1.0), jnp.broadcast_to(kept_total, (slots, LANES))],
        axis=0,
    )
    out2[...] = reply.T.reshape(nx, ny, LANES)
    exchange((mx, my), out2, mid2, got2, send2, recv2, local_sem.at[1], sizes)

    answer = got2[...].reshape(devices, LANES).T
    pieces = parts_of(answer, 3)
    kept_of = dot(pieces[0][3 * slots :], hot_group[...]) + dot(pieces[1][3 * slots :], hot_group[...])
    group_hit = iota((slots, groups), 0) == (slot_row % owned) * MOST
    kept_row = jnp.sum(jnp.where(group_hit, kept_of, 0.0), axis=0, keepdims=True)
    kept8 = jnp.concatenate(
        [kept_row[:, i * LANES : (i + 1) * LANES] for i in range(half)], axis=0
    )
    kept_parts = parts_of(kept8, 2)
    start8 = dot(kept_parts[0], upper) + dot(kept_parts[1], upper)
    row_total = jnp.sum(kept8, axis=1, keepdims=True)
    running = [jnp.zeros((1, 1), F32)]
    for i in range(half - 1):
        running.append(running[-1] + row_total[i : i + 1])
    start8 = start8 + jnp.concatenate(running, axis=0)
    start_parts = jnp.concatenate(parts_of(start8, 3), axis=0)
    start_found = dot(start_parts, hot_label[...])
    start_found = start_found[:half] + start_found[half : 2 * half] + start_found[2 * half :]
    start = jnp.sum(jnp.where(high_hit, start_found, 0.0), axis=0, keepdims=True)

    table = [piece[: 3 * slots] for piece in pieces]
    values = dot(table[0], hot_dest[...]) + dot(table[1], hot_dest[...]) + dot(table[2], hot_dest[...])
    chosen = [
        jnp.sum(jnp.where(slot_hit, values[v * slots : (v + 1) * slots], 0.0), axis=0, keepdims=True)
        for v in range(3)
    ]
    kept = chosen[2] >= 0.0
    index_ref[...] = jnp.where(kept, start + chosen[2], -1.0).astype(I32)
    pot_ref[...] = jnp.where(kept, chosen[0], 0.0)
    bind_ref[...] = jnp.where(kept, chosen[1], 0.0)


def shards(sizes, positions, velocities, masses, labels, owner_slot, group_cap):
    nx, ny = sizes
    count = masses.shape[0]
    groups = owner_slot.shape[0]
    owned = groups // (nx * ny)
    slots = owned * MOST
    vmem = pl.BlockSpec(memory_space=pltpu.VMEM)
    wide = lambda width: pltpu.VMEM((nx, ny, width), F32)
    index, pot, bind, catalog = pl.pallas_call(
        functools.partial(kernel, sizes),
        out_shape=(
            jax.ShapeDtypeStruct((1, count), I32),
            jax.ShapeDtypeStruct((1, count), F32),
            jax.ShapeDtypeStruct((1, count), F32),
            jax.ShapeDtypeStruct((4, owned), F32),
        ),
        in_specs=[vmem] * 8,
        out_specs=(vmem,) * 4,
        scratch_shapes=[
            wide(2 * LANES), wide(2 * LANES), wide(2 * LANES),
            wide(LANES), wide(LANES), wide(LANES),
            pltpu.VMEM((LANES, count), BF16),
            pltpu.VMEM((nx * ny, count), BF16),
            pltpu.VMEM((nx * ny, groups), BF16),
            pltpu.VMEM((2 * LANES, LANES), F32),
            pltpu.VMEM((slots, 8, LANES), F32),
            pltpu.SemaphoreType.DMA((nx + ny,)),
            pltpu.SemaphoreType.DMA((nx + ny,)),
            pltpu.SemaphoreType.DMA((nx + ny,)),
            pltpu.SemaphoreType.DMA((nx + ny,)),
            pltpu.SemaphoreType.DMA((2, 2)),
        ],
        compiler_params=pltpu.CompilerParams(collective_id=0, has_side_effects=True),
        name="unbind",
    )(
        labels.reshape(1, count), labels.reshape(count // LANES, LANES), positions, velocities,
        masses.reshape(1, count), owner_slot.reshape(groups // LANES, LANES),
        owner_slot.reshape(1, groups), group_cap.reshape(1, groups),
    )
    return (index.reshape(count), pot.reshape(count), bind.reshape(count), catalog)


def solution(mesh):
    sizes = (mesh.shape["gx"], mesh.shape["gy"])
    return jax.shard_map(
        functools.partial(shards, sizes),
        mesh=mesh,
        in_specs=(
            P(None, ("gx", "gy")),
            P(None, ("gx", "gy")),
            P(("gx", "gy")),
            P(("gx", "gy"), None),
            P(),
            P(),
        ),
        out_specs=(P(("gx", "gy")), P(("gx", "gy")), P(("gx", "gy")), P(None, ("gx", "gy"))),
        check_vma=False,
    )
```

```python
import functools

import jax
import jax.numpy as jnp
from jax import lax
from jax.experimental import pallas as pl
from jax.experimental.pallas import tpu as pltpu
from jax.sharding import PartitionSpec as P

CAP = 2048
SOFTENING_SQ = 0.0025
MOST = 4
LANES = 128
MESH = pl.DeviceIdType.MESH
F32, BF16, I32 = jnp.float32, jnp.bfloat16, jnp.int32


def iota(shape, axis):
    return lax.broadcasted_iota(I32, shape, axis)


def onehot(index_row, depth):
    hit = iota((depth, index_row.shape[1]), 0) == index_row
    return jnp.where(hit, 1.0, 0.0).astype(BF16)


def parts_of(value, count):
    found = []
    for step in range(count):
        part = value.astype(BF16)
        found.append(part)
        if step < count - 1:
            value = value - part.astype(F32)
    return found


def dot(left, right):
    return lax.dot_general(left, right, (((1,), (0,)), ((), ())), preferred_element_type=F32)


def dot_nt(left, right):
    return lax.dot_general(left, right, (((1,), (1,)), ((), ())), preferred_element_type=F32)


def quad_sum(value):
    lane = iota(value.shape, 1)
    for step in (1, 2):
        up = pltpu.roll(value, LANES - step, 1)
        down = pltpu.roll(value, step, 1)
        value = value + jnp.where((lane & step) == 0, up, down)
    return value


def far_first():
    ring = (0, 1, 2, 1)
    offsets = [(dz, dx, dy, dc) for dz in range(4) for dx in range(4) for dy in range(4) for dc in range(2)]
    offsets.sort(key=lambda o: (-(ring[o[0]] + ring[o[1]] + ring[o[2]]), -o[3]))
    return offsets[:-1]


def send_row(here, offset, out, got, send, recv, ny):
    mx, my = here
    dz, dx, dy, dc = offset
    px = ((mx // 4 + dz) % 4) * 4 + (mx + dx) % 4
    py = ((my // 2 + dy) % 4) * 2 + (my + dc) % 2
    pltpu.make_async_remote_copy(
        src_ref=out.at[pl.ds(px * ny + py, 1)],
        dst_ref=got.at[pl.ds(mx * ny + my, 1)],
        send_sem=send,
        recv_sem=recv,
        device_id=(px, py),
        device_id_type=MESH,
    ).start()


def kernel(
    sizes, lab_ref, lab16_ref, pos_ref, vel_ref, mass_ref, slot8_ref, slot_ref, cap_ref,
    reply_ref, place_ref, cat_ref,
    out1, spare1, got1, out2, spare2, got2, hot_dest, rows_ref, points, motion, member, halves,
    send1, recv1, send2, recv2, ready,
):
    nx, ny = sizes
    devices = nx * ny
    mx, my = lax.axis_index("gx"), lax.axis_index("gy")
    me = mx * ny + my
    count = lab_ref.shape[1]
    groups = slot_ref.shape[1]
    owned = groups // devices
    slots = owned * MOST
    blocks = count // LANES

    barrier = pltpu.get_barrier_semaphore()
    for step in range(1, ny):
        pl.semaphore_signal(barrier, inc=1, device_id=(mx, lax.rem(my + step, ny)), device_id_type=MESH)
    for step in range(1, nx):
        pl.semaphore_signal(barrier, inc=1, device_id=(lax.rem(mx + step, nx), my), device_id_type=MESH)

    label = lab_ref[...]
    label_high, label_low = label >> 7, label & 127
    slot8 = slot8_ref[...]
    table = jnp.concatenate([slot8 // owned, slot8 % owned], axis=0).astype(F32).astype(BF16)
    found = dot(table, onehot(label_low, LANES))
    high_hit = iota((groups // LANES, count), 0) == label_high
    half = groups // LANES
    dest = jnp.sum(jnp.where(high_hit, found[:half], 0.0), axis=0, keepdims=True).astype(I32)
    local_group = jnp.sum(jnp.where(high_hit, found[half:], 0.0), axis=0, keepdims=True).astype(I32)

    columns = jnp.concatenate(
        [lab16_ref[...], jnp.zeros((LANES - blocks, LANES), I32)], axis=0
    ).astype(F32).T.astype(I32)
    ranks = []
    triangle = iota((LANES, LANES), 0) < iota((LANES, LANES), 1)
    for block in range(blocks):
        mine = label[:, block * LANES : (block + 1) * LANES]
        ranks.append(jnp.zeros((8, LANES), I32))
    for other in range(blocks):
        column = jnp.broadcast_to(columns[:, other : other + 1], (LANES, LANES))
        for block in range(other, blocks):
            mine = label[:, block * LANES : (block + 1) * LANES]
            same = column == mine
            if block == other:
                same = same & triangle
            hits = jnp.where(same, 1, 0)
            ranks[block] = ranks[block] + jnp.sum(hits.reshape(LANES // 8, 8, LANES), axis=0)
    rank = jnp.concatenate([jnp.sum(r, axis=0, keepdims=True) for r in ranks], axis=1)
    slot = local_group * MOST + rank
    place_ref[...] = dest * slots + slot

    hot_dest[...] = onehot(dest, devices)
    slot_hit = iota((slots, count), 0) == slot
    fields = [mass_ref[...], pos_ref[0:1, :], pos_ref[1:2, :], pos_ref[2:3, :],
              vel_ref[0:1, :], vel_ref[1:2, :], vel_ref[2:3, :]]
    split = [[part.astype(F32) for part in parts_of(field, 3)] for field in fields]
    for half_row in range(2):
        rows = None
        for part in range(3):
            chosen = [
                jnp.where(slot_hit, split[f][part], 0.0).astype(BF16)
                for f in range(half_row * 4, min(half_row * 4 + 4, 7))
            ]
            if half_row == 1:
                chosen.append(jnp.zeros((slots, count), BF16))
            product = dot_nt(hot_dest[...], jnp.concatenate(chosen, axis=0))
            rows = product if rows is None else rows + product
        out1[:, half_row * LANES : (half_row + 1) * LANES] = rows

    slot_row = slot_ref[...]
    mine = jnp.where(iota((LANES, groups), 0) // MOST == slot_row - me * owned, 1.0, 0.0).astype(BF16)
    limits = jnp.minimum(cap_ref[...], CAP)
    limit_parts = jnp.concatenate([limits // 64, limits % 64], axis=0).astype(F32).astype(BF16)
    limit = dot_nt(limit_parts, mine)
    limit = limit[0:1] * 64.0 + limit[1:2]
    lower = jnp.where(iota((LANES, LANES), 1) < iota((LANES, LANES), 0), 1.0, 0.0).astype(BF16)
    quarter = (iota((1, LANES), 1) % MOST).astype(F32)

    pl.semaphore_wait(barrier, nx + ny - 2)
    for step in range(1, nx):
        pl.semaphore_signal(ready, inc=1, device_id=(lax.rem(mx + step, nx), my), device_id_type=MESH)
    pl.semaphore_wait(ready, nx - 1)
    here = (mx, my)
    for offset in far_first():
        send_row(here, offset, out1, got1, send1, recv1, ny)
    own = pl.ds(me, 1)
    pltpu.make_async_copy(out1.at[own], got1.at[own], recv1).start()
    pltpu.make_async_copy(out1.at[own], spare1.at[own], send1).start()
    pltpu.make_async_copy(out1, out1, send1).wait()
    pltpu.make_async_copy(got1, got1, recv1).wait()

    first = got1[:, :LANES]
    lane = iota((1, LANES), 1)
    is_mass = lane < slots
    valid = is_mass & (first > 0.0)
    tally = quad_sum(jnp.where(valid, 1.0, 0.0))
    member_rank = dot(lower, tally.astype(BF16)) + quarter
    keep = valid & (member_rank < limit)
    points[...] = jnp.where(is_mass & ~keep, 0.0, first)
    rows_ref[...] = points[...].T
    kept_mass = jnp.where(keep, first, 0.0)
    kept_total = quad_sum(jnp.sum(jnp.where(keep, 1.0, 0.0), axis=0, keepdims=True))
    mass_sum = quad_sum(jnp.sum(kept_mass, axis=0, keepdims=True))
    second = got1[:, LANES:]
    stats = [mass_sum * (1.0 / CAP)]
    energy = None
    for axis in range(3):
        speed = second if axis == 0 else pltpu.roll(second, LANES - axis * slots, 1)
        bulk = quad_sum(jnp.sum(kept_mass * speed, axis=0, keepdims=True)) / mass_sum
        stats.append(bulk)
        apart = (speed - bulk) * (speed - bulk)
        energy = apart if energy is None else energy + apart
    motion[...] = jnp.where((lane >= slots) & (lane < 2 * slots), pltpu.roll(0.5 * energy, slots, 1), 0.0)
    pick = iota((LANES, owned), 0) == iota((LANES, owned), 1) * MOST
    stat_rows = jnp.concatenate(stats + [jnp.zeros((LANES - 4, LANES), F32)], axis=0).T
    for number in range(4):
        cat_ref[number : number + 1, :] = jnp.sum(
            jnp.where(pick, stat_rows[:, number : number + 1], 0.0), axis=0, keepdims=True
        )
    rank_or_not = jnp.where(keep, member_rank, -1.0)
    member[...] = jnp.where(
        lane < 3 * slots,
        pltpu.roll(rank_or_not, 2 * slots, 1),
        pltpu.roll(jnp.broadcast_to(kept_total, (devices, LANES)), 3 * slots, 1),
    )
    offset8 = iota((8, LANES), 1) - iota((8, LANES), 0)
    lane8 = iota((8, LANES), 1)
    spot8 = lane8 % slots
    ones = jnp.ones((2 * LANES, LANES), BF16)

    def order(digit):
        half, odd = digit // 2, digit % 2
        return (1 - half) * (2 - odd) + half * (3 - 3 * odd)

    def column_of(step):
        dz, dx = order(step // 4), order(step % 4)
        return ((mx // 4 + dz) % 4) * 4 + (mx + dx) % 4

    def conclude(px):
        at = pl.ds(pl.multiple_of(px * 8, 8), 8)
        sums = dot(halves[...], ones)
        pot = jnp.zeros((8, LANES), F32)
        for spot in range(slots):
            pot = jnp.where(spot8 == spot, sums[spot * 8 : spot * 8 + 8], pot)
        both = pot * (-1.0 / CAP) + motion[at, :]
        out2[at, :] = jnp.where(lane8 < 2 * slots, both, member[at, :])

    def send_block(px):
        for peer in range(ny):

            @pl.when((px - mx) * (px - mx) + (peer - my) * (peer - my) > 0)
            def _():
                pltpu.make_async_remote_copy(
                    src_ref=out2.at[pl.ds(px * ny + peer, 1)],
                    dst_ref=got2.at[own],
                    send_sem=send2,
                    recv_sem=recv2,
                    device_id=(px, peer),
                    device_id_type=MESH,
                ).start()

    def block_of(step, carry):
        px = column_of(step)
        before = column_of((step + nx - 1) % nx)
        conclude(before)
        target = points[pl.ds(pl.multiple_of(px * 8, 8), 8), :]
        diagonal = offset8 == px * 8
        for group in range(owned):
            base = group * MOST
            there = [
                [jnp.broadcast_to(rows_ref[f * slots + base + r : f * slots + base + r + 1, :], (8, LANES)) for f in range(4)]
                for r in range(MOST)
            ]
            totals = []
            for r in range(MOST):
                spot = base + r
                px_, py_, pz_ = [
                    jnp.broadcast_to(target[:, f * slots + spot : f * slots + spot + 1], (8, LANES))
                    for f in range(1, 4)
                ]
                total = None
                for other in range(MOST):
                    ax = px_ - there[other][1]
                    ay = py_ - there[other][2]
                    az = pz_ - there[other][3]
                    inverse = lax.rsqrt(ax * ax + ay * ay + az * az + SOFTENING_SQ)
                    if r == other:
                        inverse = jnp.where(diagonal, 0.0, inverse)
                    term = inverse * there[other][0]
                    total = term if total is None else total + term
                totals.append(total)
            for pair in range(0, MOST, 2):
                two = jnp.concatenate(totals[pair : pair + 2], axis=0)
                high, low = parts_of(two, 2)
                lines = pl.ds((base + pair) * 8, 16)
                halves[lines, :LANES] = high
                halves[lines, LANES:] = low

        @pl.when(step > 0)
        def _():
            send_block(before)

        return carry

    halves[...] = jnp.zeros_like(halves)
    lax.fori_loop(0, nx, block_of, 0)
    conclude(mx)
    send_block(mx)
    pltpu.make_async_copy(out2.at[own], got2.at[own], recv2).start()
    pltpu.make_async_copy(out2.at[own], spare2.at[own], send2).start()
    pltpu.make_async_copy(out2, out2, send2).wait()
    pltpu.make_async_copy(got2, got2, recv2).wait()
    reply_ref[...] = got2[...]


def finish(lab_ref, slot_ref, place_ref, reply_ref, cat_in, index_ref, pot_ref, bind_ref, cat_ref):
    count = lab_ref.shape[1]
    groups = slot_ref.shape[1]
    devices = reply_ref.shape[0]
    half = groups // LANES
    owned = groups // devices
    slots = owned * MOST
    cat_ref[...] = cat_in[...]
    label = lab_ref[...]
    label_high, label_low = label >> 7, label & 127
    high_hit = iota((half, count), 0) == label_high
    place = place_ref[...]
    hot_dest = onehot(place // slots, devices)
    slot_hit = iota((slots, count), 0) == place % slots
    slot_row = slot_ref[...]
    hot_group = onehot(slot_row // owned, devices)
    upper = jnp.where(iota((LANES, LANES), 0) < iota((LANES, LANES), 1), 1.0, 0.0).astype(BF16)

    answer = reply_ref[...].T
    pieces = parts_of(answer, 3)
    kept_of = dot(pieces[0][3 * slots :], hot_group) + dot(pieces[1][3 * slots :], hot_group)
    group_hit = iota((slots, groups), 0) == (slot_row % owned) * MOST
    kept_row = jnp.sum(jnp.where(group_hit, kept_of, 0.0), axis=0, keepdims=True)
    kept8 = jnp.concatenate(
        [kept_row[:, i * LANES : (i + 1) * LANES] for i in range(half)], axis=0
    )
    kept_parts = parts_of(kept8, 2)
    start8 = dot(kept_parts[0], upper) + dot(kept_parts[1], upper)
    row_total = jnp.sum(kept8, axis=1, keepdims=True)
    running = [jnp.zeros((1, 1), F32)]
    for i in range(half - 1):
        running.append(running[-1] + row_total[i : i + 1])
    start8 = start8 + jnp.concatenate(running, axis=0)
    start_parts = jnp.concatenate(parts_of(start8, 3), axis=0)
    start_found = dot(start_parts, onehot(label_low, LANES))
    start_found = start_found[:half] + start_found[half : 2 * half] + start_found[2 * half :]
    start = jnp.sum(jnp.where(high_hit, start_found, 0.0), axis=0, keepdims=True)

    table = [piece[: 3 * slots] for piece in pieces]
    values = dot(table[0], hot_dest) + dot(table[1], hot_dest) + dot(table[2], hot_dest)
    chosen = [
        jnp.sum(jnp.where(slot_hit, values[v * slots : (v + 1) * slots], 0.0), axis=0, keepdims=True)
        for v in range(3)
    ]
    kept = chosen[2] >= 0.0
    index_ref[...] = jnp.where(kept, start + chosen[2], -1.0).astype(I32)
    pot_ref[...] = jnp.where(kept, chosen[0], 0.0)
    bind_ref[...] = jnp.where(kept, chosen[1], 0.0)


def shards(sizes, positions, velocities, masses, labels, owner_slot, group_cap):
    nx, ny = sizes
    count = masses.shape[0]
    groups = owner_slot.shape[0]
    owned = groups // (nx * ny)
    slots = owned * MOST
    vmem = pl.BlockSpec(memory_space=pltpu.VMEM)
    devices = nx * ny
    wide = lambda width: pltpu.VMEM((devices, width), F32)
    label_row = labels.reshape(1, count)
    slot_row = owner_slot.reshape(1, groups)
    reply, place, catalog = pl.pallas_call(
        functools.partial(kernel, sizes),
        out_shape=(
            jax.ShapeDtypeStruct((devices, LANES), F32),
            jax.ShapeDtypeStruct((1, count), I32),
            jax.ShapeDtypeStruct((4, owned), F32),
        ),
        in_specs=[vmem] * 8,
        out_specs=(vmem,) * 3,
        scratch_shapes=[
            *[wide(2 * LANES)] * 3,
            *[wide(LANES)] * 3,
            pltpu.VMEM((devices, count), BF16),
            *[wide(LANES)] * 4,
            pltpu.VMEM((slots * 8, 2 * LANES), BF16),
            *[pltpu.SemaphoreType.DMA] * 4,
            pltpu.SemaphoreType.REGULAR,
        ],
        compiler_params=pltpu.CompilerParams(collective_id=0, has_side_effects=True),
        name="unbind",
    )(
        label_row, labels.reshape(count // LANES, LANES), positions, velocities,
        masses.reshape(1, count), owner_slot.reshape(groups // LANES, LANES),
        slot_row, group_cap.reshape(1, groups),
    )
    row = lambda dtype: jax.ShapeDtypeStruct((1, count), dtype)
    index, pot, bind, catalog = pl.pallas_call(
        finish,
        out_shape=(row(I32), row(F32), row(F32), jax.ShapeDtypeStruct((4, owned), F32)),
        in_specs=[vmem] * 5,
        out_specs=(vmem,) * 4,
        name="finish",
    )(label_row, slot_row, place, reply, catalog)
    return (index.reshape(count), pot.reshape(count), bind.reshape(count), catalog)


def solution(mesh):
    sizes = (mesh.shape["gx"], mesh.shape["gy"])
    return jax.shard_map(
        functools.partial(shards, sizes),
        mesh=mesh,
        in_specs=(
            P(None, ("gx", "gy")),
            P(None, ("gx", "gy")),
            P(("gx", "gy")),
            P(("gx", "gy"), None),
            P(),
            P(),
        ),
        out_specs=(P(("gx", "gy")), P(("gx", "gy")), P(("gx", "gy")), P(None, ("gx", "gy"))),
        check_vma=False,
    )
```

```python
import functools

import jax
import jax.numpy as jnp
from jax import lax
from jax.experimental import pallas as pl
from jax.experimental.pallas import tpu as pltpu
from jax.sharding import PartitionSpec as P

CAP = 2048
SOFTENING_SQ = 0.0025
MOST = 4
LANES = 128
MESH = pl.DeviceIdType.MESH
F32, BF16, I32 = jnp.float32, jnp.bfloat16, jnp.int32


def iota(shape, axis):
    return lax.broadcasted_iota(I32, shape, axis)


def onehot(index_row, depth):
    hit = iota((depth, index_row.shape[1]), 0) == index_row
    return jnp.where(hit, 1.0, 0.0).astype(BF16)


def parts_of(value, count):
    found = []
    for step in range(count):
        part = value.astype(BF16)
        found.append(part)
        if step < count - 1:
            value = value - part.astype(F32)
    return found


def pick_lanes(table, index_row):
    found = []
    for at in range(0, index_row.shape[1], LANES):
        index = jnp.broadcast_to(index_row[:, at : at + LANES], (8, LANES))
        found.append(jnp.concatenate([
            jnp.take_along_axis(table[row : row + 8], index, axis=1)
            for row in range(0, table.shape[0], 8)
        ], axis=0))
    return jnp.concatenate(found, axis=1)


def dot(left, right):
    return lax.dot_general(left, right, (((1,), (0,)), ((), ())), preferred_element_type=F32)


def dot_nt(left, right):
    return lax.dot_general(left, right, (((1,), (1,)), ((), ())), preferred_element_type=F32)


def quad_sum(value):
    lane = iota(value.shape, 1)
    for step in (1, 2):
        up = pltpu.roll(value, LANES - step, 1)
        down = pltpu.roll(value, step, 1)
        value = value + jnp.where((lane & step) == 0, up, down)
    return value


def far_first():
    ring = (0, 1, 2, 1)
    offsets = [(dz, dx, dy, dc) for dz in range(4) for dx in range(4) for dy in range(4) for dc in range(2)]
    offsets.sort(key=lambda o: (-(ring[o[0]] + ring[o[1]] + ring[o[2]]), -o[3]))
    return offsets[:-1]


def send_row(here, offset, out, got, send, recv, ny):
    mx, my = here
    dz, dx, dy, dc = offset
    px = ((mx // 4 + dz) % 4) * 4 + (mx + dx) % 4
    py = ((my // 2 + dy) % 4) * 2 + (my + dc) % 2
    pltpu.make_async_remote_copy(
        src_ref=out.at[pl.ds(px * ny + py, 1)],
        dst_ref=got.at[pl.ds(mx * ny + my, 1)],
        send_sem=send,
        recv_sem=recv,
        device_id=(px, py),
        device_id_type=MESH,
    ).start()


def kernel(
    sizes, lab_hbm, lab16_hbm, pos_hbm, vel_hbm, mass_hbm, slot8_hbm, slot_hbm, cap_hbm,
    index_ref, pot_ref, bind_ref, cat_ref,
    lab_ref, lab16_ref, pos_ref, vel_ref, mass_ref, slot8_ref, slot_ref, cap_ref,
    out1, spare1, got1, out2, spare2, got2, hot_dest,
    rows_ref, points, motion, member, halves,
    load_sems, send1, recv1, send2, recv2, ready,
):
    nx, ny = sizes
    devices = nx * ny
    mx, my = lax.axis_index("gx"), lax.axis_index("gy")
    me = mx * ny + my
    count = lab_ref.shape[1]
    groups = slot_ref.shape[1]
    owned = groups // devices
    slots = owned * MOST
    blocks = count // LANES
    half = groups // LANES

    loads = [
        pltpu.make_async_copy(source, place, load_sems.at[number])
        for number, (source, place) in enumerate((
            (lab_hbm, lab_ref), (slot8_hbm, slot8_ref), (lab16_hbm, lab16_ref), (mass_hbm, mass_ref),
            (pos_hbm, pos_ref), (vel_hbm, vel_ref), (slot_hbm, slot_ref), (cap_hbm, cap_ref),
        ))
    ]
    for load in loads:
        load.start()
    barrier = pltpu.get_barrier_semaphore()
    for step in range(1, nx):
        pl.semaphore_signal(barrier, inc=1, device_id=(lax.rem(mx + step, nx), my), device_id_type=MESH)
    for step in range(1, ny):
        pl.semaphore_signal(barrier, inc=1, device_id=(mx, lax.rem(my + step, ny)), device_id_type=MESH)
    for load in loads:
        load.wait()

    label = lab_ref[...]
    label_high, label_low = label >> 7, label & 127
    slot8 = slot8_ref[...]
    table = jnp.concatenate([slot8 // owned, slot8 % owned], axis=0).astype(F32).astype(BF16)
    high_hit = iota((half, count), 0) == label_high
    owner = jnp.sum(
        jnp.where(high_hit, pick_lanes(slot8_ref[...], label_low), 0), axis=0, keepdims=True
    )
    dest, local_group = owner // owned, owner % owned

    columns = jnp.concatenate(
        [lab16_ref[...], jnp.zeros((LANES - blocks, LANES), I32)], axis=0
    ).astype(F32).T.astype(I32)
    ranks = []
    triangle = iota((LANES, LANES), 0) < iota((LANES, LANES), 1)
    for block in range(blocks):
        mine = label[:, block * LANES : (block + 1) * LANES]
        ranks.append(jnp.zeros((8, LANES), I32))
    for other in range(blocks):
        column = jnp.broadcast_to(columns[:, other : other + 1], (LANES, LANES))
        for block in range(other, blocks):
            mine = label[:, block * LANES : (block + 1) * LANES]
            same = column == mine
            if block == other:
                same = same & triangle
            hits = jnp.where(same, 1, 0)
            ranks[block] = ranks[block] + jnp.sum(hits.reshape(LANES // 8, 8, LANES), axis=0)
    rank = jnp.concatenate([jnp.sum(r, axis=0, keepdims=True) for r in ranks], axis=1)
    slot = local_group * MOST + rank

    hot_dest[...] = onehot(dest, devices)
    slot_hit = iota((slots, count), 0) == slot
    fields = [mass_ref[...], pos_ref[0:1, :], pos_ref[1:2, :], pos_ref[2:3, :],
              vel_ref[0:1, :], vel_ref[1:2, :], vel_ref[2:3, :]]
    split = [[part.astype(F32) for part in parts_of(field, 3)] for field in fields]
    for half_row in range(2):
        rows = None
        for part in range(3):
            chosen = [
                jnp.where(slot_hit, split[f][part], 0.0).astype(BF16)
                for f in range(half_row * 4, min(half_row * 4 + 4, 7))
            ]
            if half_row == 1:
                chosen.append(jnp.zeros((slots, count), BF16))
            product = dot_nt(hot_dest[...], jnp.concatenate(chosen, axis=0))
            rows = product if rows is None else rows + product
        out1[:, half_row * LANES : (half_row + 1) * LANES] = rows

    slot_row = slot_ref[...]
    mine = jnp.where(iota((LANES, groups), 0) // MOST == slot_row - me * owned, 1.0, 0.0).astype(BF16)
    limits = jnp.minimum(cap_ref[...], CAP)
    limit_parts = jnp.concatenate([limits // 64, limits % 64], axis=0).astype(F32).astype(BF16)
    limit = dot_nt(limit_parts, mine)
    limit = limit[0:1] * 64.0 + limit[1:2]
    lower = jnp.where(iota((LANES, LANES), 1) < iota((LANES, LANES), 0), 1.0, 0.0).astype(BF16)
    quarter = (iota((1, LANES), 1) % MOST).astype(F32)

    pl.semaphore_wait(barrier, nx + ny - 2)
    for step in range(1, ny):
        pl.semaphore_signal(ready, inc=1, device_id=(mx, lax.rem(my + step, ny)), device_id_type=MESH)
    pl.semaphore_wait(ready, ny - 1)
    here = (mx, my)
    for offset in far_first():
        send_row(here, offset, out1, got1, send1, recv1, ny)
    own = pl.ds(me, 1)
    pltpu.make_async_copy(out1.at[own], got1.at[own], recv1).start()
    pltpu.make_async_copy(out1.at[own], spare1.at[own], send1).start()
    pltpu.make_async_copy(out1, out1, send1).wait()
    pltpu.make_async_copy(got1, got1, recv1).wait()

    first = got1[:, :LANES]
    lane = iota((1, LANES), 1)
    is_mass = lane < slots
    valid = is_mass & (first > 0.0)
    tally = quad_sum(jnp.where(valid, 1.0, 0.0))
    member_rank = dot(lower, tally.astype(BF16)) + quarter
    keep = valid & (member_rank < limit)
    points[...] = jnp.where(is_mass & ~keep, 0.0, first)
    rows_ref[...] = points[...].T
    kept_mass = jnp.where(keep, first, 0.0)
    kept_total = quad_sum(jnp.sum(jnp.where(keep, 1.0, 0.0), axis=0, keepdims=True))
    mass_sum = quad_sum(jnp.sum(kept_mass, axis=0, keepdims=True))
    second = got1[:, LANES:]
    stats = [mass_sum * (1.0 / CAP)]
    energy = None
    for axis in range(3):
        speed = second if axis == 0 else pltpu.roll(second, LANES - axis * slots, 1)
        bulk = quad_sum(jnp.sum(kept_mass * speed, axis=0, keepdims=True)) / mass_sum
        stats.append(bulk)
        apart = (speed - bulk) * (speed - bulk)
        energy = apart if energy is None else energy + apart
    motion[...] = jnp.where((lane >= slots) & (lane < 2 * slots), pltpu.roll(0.5 * energy, slots, 1), 0.0)
    rank_or_not = jnp.where(keep, member_rank, -1.0)
    member[...] = jnp.where(
        lane < 3 * slots,
        pltpu.roll(rank_or_not, 2 * slots, 1),
        jnp.broadcast_to(
            jnp.take_along_axis(
                jnp.broadcast_to(kept_total, (8, LANES)), (iota((8, LANES), 1) % owned) * MOST, axis=1
            )[0:1],
            (devices, LANES),
        ),
    )
    offset8 = iota((8, LANES), 1) - iota((8, LANES), 0)
    lane8 = iota((8, LANES), 1)
    spot8 = lane8 % slots
    ones = jnp.ones((2 * LANES, LANES), BF16)

    def order(digit):
        half, odd = digit // 2, digit % 2
        return (1 - half) * (2 - odd) + half * (3 - 3 * odd)

    def column_of(step):
        dz, dx = order(step // 4), order(step % 4)
        return ((mx // 4 + dz) % 4) * 4 + (mx + dx) % 4

    def conclude(px):
        at = pl.ds(pl.multiple_of(px * 8, 8), 8)
        sums = dot(halves[...], ones)
        pot = jnp.zeros((8, LANES), F32)
        for spot in range(slots):
            pot = jnp.where(spot8 == spot, sums[spot * 8 : spot * 8 + 8], pot)
        both = pot * (-1.0 / CAP) + motion[at, :]
        out2[at, :] = jnp.where(lane8 < 2 * slots, both, member[at, :])

    def send_to(px, peer):
        pltpu.make_async_remote_copy(
            src_ref=out2.at[pl.ds(px * ny + peer, 1)],
            dst_ref=got2.at[own],
            send_sem=send2,
            recv_sem=recv2,
            device_id=(px, peer),
            device_id_type=MESH,
        ).start()

    def pairs_of(px, between):
        target = points[pl.ds(pl.multiple_of(px * 8, 8), 8), :]
        diagonal = offset8 == px * 8
        for group in range(owned):
            if group == owned // 2:
                between()
            base = group * MOST
            there = [
                [jnp.broadcast_to(rows_ref[f * slots + base + r : f * slots + base + r + 1, :], (8, LANES)) for f in range(4)]
                for r in range(MOST)
            ]
            totals = []
            for r in range(MOST):
                spot = base + r
                px_, py_, pz_ = [
                    jnp.broadcast_to(target[:, f * slots + spot : f * slots + spot + 1], (8, LANES))
                    for f in range(1, 4)
                ]
                total = None
                for other in range(MOST):
                    ax = px_ - there[other][1]
                    ay = py_ - there[other][2]
                    az = pz_ - there[other][3]
                    inverse = lax.rsqrt(ax * ax + ay * ay + az * az + SOFTENING_SQ)
                    if r == other:
                        inverse = jnp.where(diagonal, 0.0, inverse)
                    term = inverse * there[other][0]
                    total = term if total is None else total + term
                totals.append(total)
            for pair in range(0, MOST, 2):
                two = jnp.concatenate(totals[pair : pair + 2], axis=0)
                high, low = parts_of(two, 2)
                lines = pl.ds((base + pair) * 8, 16)
                halves[lines, :LANES] = high
                halves[lines, LANES:] = low

    def block_of(turn, carry):
        gone = []
        for piece in range(3):
            step = turn * 3 + piece + 1
            before = column_of(step - 1)
            conclude(before)
            pairs_of(column_of(step), lambda: None)
            gone.append(before)
            if False:
                for peer in range(ny):
                    send_to(before, peer)
        if not False:
            for before in gone:
                for peer in range(ny):
                    send_to(before, peer)
        return carry

    pairs_of(column_of(0), lambda: None)
    lax.fori_loop(0, (nx - 1) // 3, block_of, 0)
    conclude(mx)
    for step in range(1, ny):
        send_to(mx, lax.rem(my + step, ny))
    pltpu.make_async_copy(out2.at[own], got2.at[own], recv2).start()
    pltpu.make_async_copy(out2.at[own], spare2.at[own], send2).start()
    pick = iota((LANES, owned), 0) == iota((LANES, owned), 1) * MOST
    stat_rows = jnp.concatenate(stats + [jnp.zeros((LANES - 4, LANES), F32)], axis=0).T
    for number in range(4):
        cat_ref[number : number + 1, :] = jnp.sum(
            jnp.where(pick, stat_rows[:, number : number + 1], 0.0), axis=0, keepdims=True
        )
    upper = jnp.where(iota((LANES, LANES), 0) < iota((LANES, LANES), 1), 1.0, 0.0).astype(BF16)
    pltpu.make_async_copy(out2, out2, send2).wait()
    pltpu.make_async_copy(got2, got2, recv2).wait()
    answer = got2[...].T
    kept_of = pick_lanes(answer[3 * slots : 3 * slots + owned], slot_row // owned)
    kept_row = jnp.sum(
        jnp.where(iota((owned, groups), 0) == slot_row % owned, kept_of, 0.0), axis=0, keepdims=True
    )
    kept8 = jnp.concatenate(
        [kept_row[:, i * LANES : (i + 1) * LANES] for i in range(half)], axis=0
    )
    kept_parts = parts_of(kept8, 2)
    start8 = dot(kept_parts[0], upper) + dot(kept_parts[1], upper)
    row_total = jnp.sum(kept8, axis=1, keepdims=True)
    running = [jnp.zeros((1, 1), F32)]
    for i in range(half - 1):
        running.append(running[-1] + row_total[i : i + 1])
    start8 = start8 + jnp.concatenate(running, axis=0)
    start = jnp.sum(jnp.where(high_hit, pick_lanes(start8, label_low), 0.0), axis=0, keepdims=True)
    chosen = [
        jnp.sum(
            jnp.where(slot_hit, pick_lanes(answer[v * slots : (v + 1) * slots], dest), 0.0),
            axis=0, keepdims=True,
        )
        for v in range(3)
    ]
    kept = chosen[2] >= 0.0
    index_ref[...] = jnp.where(kept, start + chosen[2], -1.0).astype(I32)
    pot_ref[...] = jnp.where(kept, chosen[0], 0.0)
    bind_ref[...] = jnp.where(kept, chosen[1], 0.0)


def finish(*refs):
    half = len(refs) // 2
    for source, result in zip(refs[:half], refs[half:]):
        result[...] = source[...]


def shards(sizes, positions, velocities, masses, labels, owner_slot, group_cap):
    nx, ny = sizes
    count = masses.shape[0]
    groups = owner_slot.shape[0]
    owned = groups // (nx * ny)
    slots = owned * MOST
    vmem = pl.BlockSpec(memory_space=pltpu.VMEM)
    devices = nx * ny
    wide = lambda width: pltpu.VMEM((devices, width), F32)
    label_row = labels.reshape(1, count)
    slot_row = owner_slot.reshape(1, groups)
    row = lambda dtype: jax.ShapeDtypeStruct((1, count), dtype)
    results = (row(I32), row(F32), row(F32), jax.ShapeDtypeStruct((4, owned), F32))
    inputs = (
        label_row, labels.reshape(count // LANES, LANES), positions, velocities,
        masses.reshape(1, count), owner_slot.reshape(groups // LANES, LANES),
        slot_row, group_cap.reshape(1, groups),
    )
    found = pl.pallas_call(
        functools.partial(kernel, sizes),
        out_shape=results,
        in_specs=[pl.BlockSpec(memory_space=pl.ANY)] * 8,
        out_specs=(vmem,) * 4,
        scratch_shapes=[
            *[pltpu.VMEM(array.shape, array.dtype) for array in inputs],
            *[wide(2 * LANES)] * 3,
            *[wide(LANES)] * 3,
            pltpu.VMEM((devices, count), BF16),
            *[wide(LANES)] * 4,
            pltpu.VMEM((slots * 8, 2 * LANES), BF16),
            pltpu.SemaphoreType.DMA((8,)),
            *[pltpu.SemaphoreType.DMA] * 4,
            pltpu.SemaphoreType.REGULAR,
        ],
        compiler_params=pltpu.CompilerParams(collective_id=0, has_side_effects=True),
        name="unbind",
    )(*inputs)
    index, pot, bind, catalog = pl.pallas_call(
        finish,
        out_shape=results,
        in_specs=[vmem] * 4,
        out_specs=(vmem,) * 4,
        name="finish",
    )(*found)
    return (index.reshape(count), pot.reshape(count), bind.reshape(count), catalog)


def solution(mesh):
    sizes = (mesh.shape["gx"], mesh.shape["gy"])
    return jax.shard_map(
        functools.partial(shards, sizes),
        mesh=mesh,
        in_specs=(
            P(None, ("gx", "gy")),
            P(None, ("gx", "gy")),
            P(("gx", "gy")),
            P(("gx", "gy"), None),
            P(),
            P(),
        ),
        out_specs=(P(("gx", "gy")), P(("gx", "gy")), P(("gx", "gy")), P(None, ("gx", "gy"))),
        check_vma=False,
    )
```

```python
import functools

import jax
import jax.numpy as jnp
from jax import lax
from jax.experimental import pallas as pl
from jax.experimental.pallas import tpu as pltpu
from jax.sharding import PartitionSpec as P

CAP = 2048
SOFTENING_SQ = 0.0025
MOST = 4
LANES = 128
MESH = pl.DeviceIdType.MESH
F32, BF16, I32 = jnp.float32, jnp.bfloat16, jnp.int32


def iota(shape, axis):
    return lax.broadcasted_iota(I32, shape, axis)


def onehot(index_row, depth):
    hit = iota((depth, index_row.shape[1]), 0) == index_row
    return jnp.where(hit, 1.0, 0.0).astype(BF16)


def parts_of(value, count):
    found = []
    for step in range(count):
        part = value.astype(BF16)
        found.append(part)
        if step < count - 1:
            value = value - part.astype(F32)
    return found


def pick_lanes(table, index_row):
    found = []
    for at in range(0, index_row.shape[1], LANES):
        index = jnp.broadcast_to(index_row[:, at : at + LANES], (8, LANES))
        found.append(jnp.concatenate([
            jnp.take_along_axis(table[row : row + 8], index, axis=1)
            for row in range(0, table.shape[0], 8)
        ], axis=0))
    return jnp.concatenate(found, axis=1)


def dot(left, right):
    return lax.dot_general(left, right, (((1,), (0,)), ((), ())), preferred_element_type=F32)


def dot_nt(left, right):
    return lax.dot_general(left, right, (((1,), (1,)), ((), ())), preferred_element_type=F32)


def quad_sum(value):
    lane = iota(value.shape, 1)
    for step in (1, 2):
        up = pltpu.roll(value, LANES - step, 1)
        down = pltpu.roll(value, step, 1)
        value = value + jnp.where((lane & step) == 0, up, down)
    return value


def far_first():
    ring = (0, 1, 2, 1)
    offsets = [(dz, dx, dy, dc) for dz in range(4) for dx in range(4) for dy in range(4) for dc in range(2)]
    offsets.sort(key=lambda o: (-(ring[o[0]] + ring[o[1]] + ring[o[2]]), -o[3]))
    return offsets[:-1]


def send_row(here, offset, out, got, send, recv, ny):
    mx, my = here
    dz, dx, dy, dc = offset
    px = ((mx // 4 + dz) % 4) * 4 + (mx + dx) % 4
    py = ((my // 2 + dy) % 4) * 2 + (my + dc) % 2
    pltpu.make_async_remote_copy(
        src_ref=out.at[pl.ds(px * ny + py, 1)],
        dst_ref=got.at[pl.ds(mx * ny + my, 1)],
        send_sem=send,
        recv_sem=recv,
        device_id=(px, py),
        device_id_type=MESH,
    ).start()


def kernel(
    sizes, lab_hbm, lab16_hbm, pos_hbm, vel_hbm, mass_hbm, slot8_hbm, slot_hbm, cap_hbm,
    index_ref, pot_ref, bind_ref, cat_ref,
    lab_ref, lab16_ref, pos_ref, vel_ref, mass_ref, slot8_ref, slot_ref, cap_ref,
    out1, spare1, got1, out2, spare2, got2, hot_dest,
    rows_ref, points, motion, member, halves,
    load_sems, send1, recv1, send2, recv2, ready,
):
    nx, ny = sizes
    devices = nx * ny
    mx, my = lax.axis_index("gx"), lax.axis_index("gy")
    me = mx * ny + my
    count = lab_ref.shape[1]
    groups = slot_ref.shape[1]
    owned = groups // devices
    slots = owned * MOST
    blocks = count // LANES
    half = groups // LANES

    loads = [
        pltpu.make_async_copy(source, place, load_sems.at[number])
        for number, (source, place) in enumerate((
            (lab_hbm, lab_ref), (slot8_hbm, slot8_ref), (lab16_hbm, lab16_ref), (mass_hbm, mass_ref),
            (pos_hbm, pos_ref), (vel_hbm, vel_ref), (slot_hbm, slot_ref), (cap_hbm, cap_ref),
        ))
    ]
    for load in loads:
        load.start()
    barrier = pltpu.get_barrier_semaphore()
    here = (mx, my)

    def announce(offsets):
        for dz, dx, dy, dc in offsets:
            px = ((mx // 4 + dz) % 4) * 4 + (mx + dx) % 4
            py = ((my // 2 + dy) % 4) * 2 + (my + dc) % 2
            pl.semaphore_signal(barrier, inc=1, device_id=(px, py), device_id_type=MESH)

    announce(far_first())
    for load in loads:
        load.wait()

    label = lab_ref[...]
    label_high, label_low = label >> 7, label & 127
    slot8 = slot8_ref[...]
    table = jnp.concatenate([slot8 // owned, slot8 % owned], axis=0).astype(F32).astype(BF16)
    high_hit = iota((half, count), 0) == label_high
    owner = jnp.sum(
        jnp.where(high_hit, pick_lanes(slot8_ref[...], label_low), 0), axis=0, keepdims=True
    )
    dest, local_group = owner // owned, owner % owned

    columns = jnp.concatenate(
        [lab16_ref[...], jnp.zeros((LANES - blocks, LANES), I32)], axis=0
    ).astype(F32).T.astype(I32)
    ranks = []
    triangle = iota((LANES, LANES), 0) < iota((LANES, LANES), 1)
    for block in range(blocks):
        mine = label[:, block * LANES : (block + 1) * LANES]
        ranks.append(jnp.zeros((8, LANES), I32))
    for other in range(blocks):
        column = jnp.broadcast_to(columns[:, other : other + 1], (LANES, LANES))
        for block in range(other, blocks):
            mine = label[:, block * LANES : (block + 1) * LANES]
            same = column == mine
            if block == other:
                same = same & triangle
            hits = jnp.where(same, 1, 0)
            ranks[block] = ranks[block] + jnp.sum(hits.reshape(LANES // 8, 8, LANES), axis=0)
    rank = jnp.concatenate([jnp.sum(r, axis=0, keepdims=True) for r in ranks], axis=1)
    slot = local_group * MOST + rank

    hot_dest[...] = onehot(dest, devices)
    slot_hit = iota((slots, count), 0) == slot
    fields = [mass_ref[...], pos_ref[0:1, :], pos_ref[1:2, :], pos_ref[2:3, :],
              vel_ref[0:1, :], vel_ref[1:2, :], vel_ref[2:3, :]]
    split = [[part.astype(F32) for part in parts_of(field, 3)] for field in fields]
    for half_row in range(2):
        rows = None
        for part in range(3):
            chosen = [
                jnp.where(slot_hit, split[f][part], 0.0).astype(BF16)
                for f in range(half_row * 4, min(half_row * 4 + 4, 7))
            ]
            if half_row == 1:
                chosen.append(jnp.zeros((slots, count), BF16))
            product = dot_nt(hot_dest[...], jnp.concatenate(chosen, axis=0))
            rows = product if rows is None else rows + product
        out1[:, half_row * LANES : (half_row + 1) * LANES] = rows

    slot_row = slot_ref[...]
    mine = jnp.where(iota((LANES, groups), 0) // MOST == slot_row - me * owned, 1.0, 0.0).astype(BF16)
    limits = jnp.minimum(cap_ref[...], CAP)
    limit_parts = jnp.concatenate([limits // 64, limits % 64], axis=0).astype(F32).astype(BF16)
    limit = dot_nt(limit_parts, mine)
    limit = limit[0:1] * 64.0 + limit[1:2]
    lower = jnp.where(iota((LANES, LANES), 1) < iota((LANES, LANES), 0), 1.0, 0.0).astype(BF16)
    quarter = (iota((1, LANES), 1) % MOST).astype(F32)

    pl.semaphore_wait(barrier, devices - 1)
    here = (mx, my)
    for offset in far_first():
        send_row(here, offset, out1, got1, send1, recv1, ny)
    own = pl.ds(me, 1)
    pltpu.make_async_copy(out1.at[own], got1.at[own], recv1).start()
    pltpu.make_async_copy(out1.at[own], spare1.at[own], send1).start()
    pltpu.make_async_copy(out1, out1, send1).wait()
    pltpu.make_async_copy(got1, got1, recv1).wait()

    first = got1[:, :LANES]
    lane = iota((1, LANES), 1)
    is_mass = lane < slots
    valid = is_mass & (first > 0.0)
    tally = quad_sum(jnp.where(valid, 1.0, 0.0))
    member_rank = dot(lower, tally.astype(BF16)) + quarter
    keep = valid & (member_rank < limit)
    points[...] = jnp.where(is_mass & ~keep, 0.0, first)
    rows_ref[...] = points[...].T
    kept_mass = jnp.where(keep, first, 0.0)
    kept_total = quad_sum(jnp.sum(jnp.where(keep, 1.0, 0.0), axis=0, keepdims=True))
    mass_sum = quad_sum(jnp.sum(kept_mass, axis=0, keepdims=True))
    second = got1[:, LANES:]
    stats = [mass_sum * (1.0 / CAP)]
    energy = None
    for axis in range(3):
        speed = second if axis == 0 else pltpu.roll(second, LANES - axis * slots, 1)
        bulk = quad_sum(jnp.sum(kept_mass * speed, axis=0, keepdims=True)) / mass_sum
        stats.append(bulk)
        apart = (speed - bulk) * (speed - bulk)
        energy = apart if energy is None else energy + apart
    motion[...] = jnp.where((lane >= slots) & (lane < 2 * slots), pltpu.roll(0.5 * energy, slots, 1), 0.0)
    rank_or_not = jnp.where(keep, member_rank, -1.0)
    member[...] = jnp.where(
        lane < 3 * slots,
        pltpu.roll(rank_or_not, 2 * slots, 1),
        jnp.broadcast_to(
            jnp.take_along_axis(
                jnp.broadcast_to(kept_total, (8, LANES)), (iota((8, LANES), 1) % owned) * MOST, axis=1
            )[0:1],
            (devices, LANES),
        ),
    )
    offset8 = iota((8, LANES), 1) - iota((8, LANES), 0)
    lane8 = iota((8, LANES), 1)
    spot8 = lane8 % slots
    ones = jnp.ones((2 * LANES, LANES), BF16)

    def order(digit):
        half, odd = digit // 2, digit % 2
        return (1 - half) * (2 - odd) + half * (3 - 3 * odd)

    def column_of(step):
        dz, dx = order(step // 4), order(step % 4)
        return ((mx // 4 + dz) % 4) * 4 + (mx + dx) % 4

    def conclude(px):
        at = pl.ds(pl.multiple_of(px * 8, 8), 8)
        sums = dot(halves[...], ones)
        pot = jnp.zeros((8, LANES), F32)
        for spot in range(slots):
            pot = jnp.where(spot8 == spot, sums[spot * 8 : spot * 8 + 8], pot)
        both = pot * (-1.0 / CAP) + motion[at, :]
        out2[at, :] = jnp.where(lane8 < 2 * slots, both, member[at, :])

    def send_to(px, peer):
        pltpu.make_async_remote_copy(
            src_ref=out2.at[pl.ds(px * ny + peer, 1)],
            dst_ref=got2.at[own],
            send_sem=send2,
            recv_sem=recv2,
            device_id=(px, peer),
            device_id_type=MESH,
        ).start()

    def pairs_of(px, between):
        target = points[pl.ds(pl.multiple_of(px * 8, 8), 8), :]
        diagonal = offset8 == px * 8
        for group in range(owned):
            if group == owned // 2:
                between()
            base = group * MOST
            there = [
                [jnp.broadcast_to(rows_ref[f * slots + base + r : f * slots + base + r + 1, :], (8, LANES)) for f in range(4)]
                for r in range(MOST)
            ]
            totals = []
            for r in range(MOST):
                spot = base + r
                px_, py_, pz_ = [
                    jnp.broadcast_to(target[:, f * slots + spot : f * slots + spot + 1], (8, LANES))
                    for f in range(1, 4)
                ]
                total = None
                for other in range(MOST):
                    ax = px_ - there[other][1]
                    ay = py_ - there[other][2]
                    az = pz_ - there[other][3]
                    inverse = lax.rsqrt(ax * ax + ay * ay + az * az + SOFTENING_SQ)
                    if r == other:
                        inverse = jnp.where(diagonal, 0.0, inverse)
                    term = inverse * there[other][0]
                    total = term if total is None else total + term
                totals.append(total)
            for pair in range(0, MOST, 2):
                two = jnp.concatenate(totals[pair : pair + 2], axis=0)
                high, low = parts_of(two, 2)
                lines = pl.ds((base + pair) * 8, 16)
                halves[lines, :LANES] = high
                halves[lines, LANES:] = low

    def block_of(turn, carry):
        gone = []
        for piece in range(3):
            step = turn * 3 + piece + 1
            before = column_of(step - 1)
            conclude(before)
            pairs_of(column_of(step), lambda: None)
            gone.append(before)
            if False:
                for peer in range(ny):
                    send_to(before, peer)
        if not False:
            for before in gone:
                for peer in range(ny):
                    send_to(before, peer)
        return carry

    pairs_of(column_of(0), lambda: None)
    lax.fori_loop(0, (nx - 1) // 3 - 1, block_of, 0)
    for step in range(nx - 3, nx):
        before = column_of(step - 1)
        conclude(before)
        for peer in range(ny):
            send_to(before, peer)
        pairs_of(column_of(step), lambda: None)
    conclude(mx)
    for step in (4, 5, 2, 3, 6, 7, 1):
        send_to(mx, lax.rem(my + step, ny))
    pltpu.make_async_copy(out2.at[own], got2.at[own], recv2).start()
    pltpu.make_async_copy(out2.at[own], spare2.at[own], send2).start()
    pick = iota((LANES, owned), 0) == iota((LANES, owned), 1) * MOST
    stat_rows = jnp.concatenate(stats + [jnp.zeros((LANES - 4, LANES), F32)], axis=0).T
    for number in range(4):
        cat_ref[number : number + 1, :] = jnp.sum(
            jnp.where(pick, stat_rows[:, number : number + 1], 0.0), axis=0, keepdims=True
        )
    upper = jnp.where(iota((LANES, LANES), 0) < iota((LANES, LANES), 1), 1.0, 0.0).astype(BF16)
    pltpu.make_async_copy(out2, out2, send2).wait()
    pltpu.make_async_copy(got2, got2, recv2).wait()
    answer = got2[...].T
    kept_of = pick_lanes(answer[3 * slots : 3 * slots + owned], slot_row // owned)
    kept_row = jnp.sum(
        jnp.where(iota((owned, groups), 0) == slot_row % owned, kept_of, 0.0), axis=0, keepdims=True
    )
    kept8 = jnp.concatenate(
        [kept_row[:, i * LANES : (i + 1) * LANES] for i in range(half)], axis=0
    )
    kept_parts = parts_of(kept8, 2)
    start8 = dot(kept_parts[0], upper) + dot(kept_parts[1], upper)
    row_total = jnp.sum(kept8, axis=1, keepdims=True)
    running = [jnp.zeros((1, 1), F32)]
    for i in range(half - 1):
        running.append(running[-1] + row_total[i : i + 1])
    start8 = start8 + jnp.concatenate(running, axis=0)
    start = jnp.sum(jnp.where(high_hit, pick_lanes(start8, label_low), 0.0), axis=0, keepdims=True)
    chosen = [
        jnp.sum(
            jnp.where(slot_hit, pick_lanes(answer[v * slots : (v + 1) * slots], dest), 0.0),
            axis=0, keepdims=True,
        )
        for v in range(3)
    ]
    kept = chosen[2] >= 0.0
    index_ref[...] = jnp.where(kept, start + chosen[2], -1.0).astype(I32)
    pot_ref[...] = jnp.where(kept, chosen[0], 0.0)
    bind_ref[...] = jnp.where(kept, chosen[1], 0.0)


def finish(*refs):
    half = len(refs) // 2
    for source, result in zip(refs[:half], refs[half:]):
        result[...] = source[...]


def shards(sizes, positions, velocities, masses, labels, owner_slot, group_cap):
    nx, ny = sizes
    count = masses.shape[0]
    groups = owner_slot.shape[0]
    owned = groups // (nx * ny)
    slots = owned * MOST
    vmem = pl.BlockSpec(memory_space=pltpu.VMEM)
    devices = nx * ny
    wide = lambda width: pltpu.VMEM((devices, width), F32)
    label_row = labels.reshape(1, count)
    slot_row = owner_slot.reshape(1, groups)
    row = lambda dtype: jax.ShapeDtypeStruct((1, count), dtype)
    results = (row(I32), row(F32), row(F32), jax.ShapeDtypeStruct((4, owned), F32))
    inputs = (
        label_row, labels.reshape(count // LANES, LANES), positions, velocities,
        masses.reshape(1, count), owner_slot.reshape(groups // LANES, LANES),
        slot_row, group_cap.reshape(1, groups),
    )
    found = pl.pallas_call(
        functools.partial(kernel, sizes),
        out_shape=results,
        in_specs=[pl.BlockSpec(memory_space=pltpu.HBM)] * 8,
        out_specs=(vmem,) * 4,
        scratch_shapes=[
            *[pltpu.VMEM(array.shape, array.dtype) for array in inputs],
            *[wide(2 * LANES)] * 3,
            *[wide(LANES)] * 3,
            pltpu.VMEM((devices, count), BF16),
            *[wide(LANES)] * 4,
            pltpu.VMEM((slots * 8, 2 * LANES), BF16),
            pltpu.SemaphoreType.DMA((8,)),
            *[pltpu.SemaphoreType.DMA] * 4,
            pltpu.SemaphoreType.REGULAR,
        ],
        compiler_params=pltpu.CompilerParams(
            collective_id=0, has_side_effects=True, vmem_limit_bytes=24 * 2**20
        ),
        name="unbind",
    )(*[pltpu.with_memory_space_constraint(array, pltpu.HBM) for array in inputs])
    index, pot, bind, catalog = pl.pallas_call(
        finish,
        out_shape=results,
        in_specs=[vmem] * 4,
        out_specs=(vmem,) * 4,
        compiler_params=pltpu.CompilerParams(vmem_limit_bytes=2**20),
        name="finish",
    )(*found)
    return (index.reshape(count), pot.reshape(count), bind.reshape(count), catalog)


def solution(mesh):
    sizes = (mesh.shape["gx"], mesh.shape["gy"])
    return jax.shard_map(
        functools.partial(shards, sizes),
        mesh=mesh,
        in_specs=(
            P(None, ("gx", "gy")),
            P(None, ("gx", "gy")),
            P(("gx", "gy")),
            P(("gx", "gy"), None),
            P(),
            P(),
        ),
        out_specs=(P(("gx", "gy")), P(("gx", "gy")), P(("gx", "gy")), P(None, ("gx", "gy"))),
        check_vma=False,
    )
```

```python
import functools

import jax
import jax.numpy as jnp
from jax import lax
from jax.experimental import pallas as pl
from jax.experimental.pallas import tpu as pltpu
from jax.sharding import PartitionSpec as P

CAP = 2048
SOFTENING_SQ = 0.0025
MOST = 4
LANES = 128
MESH = pl.DeviceIdType.MESH
F32, BF16, I32 = jnp.float32, jnp.bfloat16, jnp.int32


def iota(shape, axis):
    return lax.broadcasted_iota(I32, shape, axis)


def onehot(index_row, depth):
    hit = iota((depth, index_row.shape[1]), 0) == index_row
    return jnp.where(hit, 1.0, 0.0).astype(BF16)


def parts_of(value, count):
    found = []
    for step in range(count):
        part = value.astype(BF16)
        found.append(part)
        if step < count - 1:
            value = value - part.astype(F32)
    return found


def pick_lanes(table, index_row):
    found = []
    for at in range(0, index_row.shape[1], LANES):
        index = jnp.broadcast_to(index_row[:, at : at + LANES], (8, LANES))
        found.append(jnp.concatenate([
            jnp.take_along_axis(table[row : row + 8], index, axis=1)
            for row in range(0, table.shape[0], 8)
        ], axis=0))
    return jnp.concatenate(found, axis=1)


def dot(left, right):
    return lax.dot_general(left, right, (((1,), (0,)), ((), ())), preferred_element_type=F32)


def dot_nt(left, right):
    return lax.dot_general(left, right, (((1,), (1,)), ((), ())), preferred_element_type=F32)


def quad_sum(value):
    lane = iota(value.shape, 1)
    for step in (1, 2):
        up = pltpu.roll(value, LANES - step, 1)
        down = pltpu.roll(value, step, 1)
        value = value + jnp.where((lane & step) == 0, up, down)
    return value


def far_first():
    ring = (0, 1, 2, 1)
    offsets = [(dz, dx, dy, dc) for dz in range(4) for dx in range(4) for dy in range(4) for dc in range(2)]
    offsets.sort(key=lambda o: (-(ring[o[0]] + ring[o[1]] + ring[o[2]]), -o[3]))
    return offsets[:-1]


def near_first():
    return [(0, 0, 0, 0)] + far_first()[::-1]


def peer_at(here, offset):
    mx, my = here
    dz, dx, dy, dc = offset
    return (((mx // 4 + dz) % 4) * 4 + (mx + dx) % 4, ((my // 2 + dy) % 4) * 2 + (my + dc) % 2)


def kernel(
    sizes, lab_hbm, lab16_hbm, pos_hbm, vel_hbm, mass_hbm, slot8_hbm, slot_hbm, cap_hbm, order_hbm,
    index_ref, pot_ref, bind_ref, cat_ref,
    lab_ref, lab16_ref, pos_ref, vel_ref, mass_ref, slot8_ref, slot_ref, cap_ref, order_ref,
    out1, spare1, got1, out2, spare2, got2, hot_dest,
    rows_ref, motion, member, halves,
    load_sems, send1, recv1, send2, recv2,
):
    nx, ny = sizes
    devices = nx * ny
    mx, my = lax.axis_index("gx"), lax.axis_index("gy")
    me = mx * ny + my
    count = lab_ref.shape[1]
    groups = slot_ref.shape[1]
    owned = groups // devices
    slots = owned * MOST
    blocks = count // LANES
    half = groups // LANES

    loads = [
        pltpu.make_async_copy(source, place, load_sems.at[number])
        for number, (source, place) in enumerate((
            (lab_hbm, lab_ref), (slot8_hbm, slot8_ref), (lab16_hbm, lab16_ref), (mass_hbm, mass_ref),
            (pos_hbm, pos_ref), (vel_hbm, vel_ref), (slot_hbm, slot_ref), (cap_hbm, cap_ref), (order_hbm, order_ref),
        ))
    ]
    for load in loads:
        load.start()
    barrier = pltpu.get_barrier_semaphore()
    here = (mx, my)

    for offset in far_first():
        pl.semaphore_signal(barrier, inc=1, device_id=peer_at(here, offset), device_id_type=MESH)
    for load in loads:
        load.wait()

    label = lab_ref[...]
    label_high, label_low = label >> 7, label & 127
    slot8 = slot8_ref[...]
    table = jnp.concatenate([slot8 // owned, slot8 % owned], axis=0).astype(F32).astype(BF16)
    high_hit = iota((half, count), 0) == label_high
    owner = jnp.sum(
        jnp.where(high_hit, pick_lanes(slot8_ref[...], label_low), 0), axis=0, keepdims=True
    )
    dest, local_group = owner // owned, owner % owned

    hot_low = onehot(label_low, LANES)
    high_one = jnp.where(high_hit, 1.0, 0.0)
    none = jnp.zeros((half, LANES), F32)
    prior = jnp.concatenate([
        jnp.concatenate([
            high_one[:, other * LANES : (other + 1) * LANES] if other < block else none
            for other in range(blocks)
        ], axis=1)
        for block in range(blocks)
    ], axis=0).astype(BF16)
    tables = dot_nt(prior, hot_low)
    columns = jnp.concatenate(
        [lab16_ref[...], jnp.zeros((LANES - blocks, LANES), I32)], axis=0
    ).astype(F32).T.astype(I32)
    triangle = jnp.where(iota((LANES, LANES), 0) < iota((LANES, LANES), 1), 1.0, 0.0)
    ranks = []
    for block in range(blocks):
        lanes = slice(block * LANES, (block + 1) * LANES)
        column = jnp.broadcast_to(columns[:, block : block + 1], (LANES, LANES))
        within = jnp.where(column == label[:, lanes], triangle, 0.0)
        before = jnp.where(
            high_hit[:, lanes], pick_lanes(tables[block * half : (block + 1) * half], label_low[:, lanes]), 0.0
        )
        within = jnp.sum(within.reshape(LANES // half, half, LANES), axis=0)
        ranks.append(jnp.sum(before + within, axis=0, keepdims=True))
    rank = jnp.concatenate(ranks, axis=1).astype(I32)
    slot = local_group * MOST + rank

    hot_dest[...] = onehot(dest, devices)
    slot_hit = iota((slots, count), 0) == slot
    fields = [mass_ref[...], pos_ref[0:1, :], pos_ref[1:2, :], pos_ref[2:3, :],
              vel_ref[0:1, :], vel_ref[1:2, :], vel_ref[2:3, :]]
    split = [[part.astype(F32) for part in parts_of(field, 3)] for field in fields]
    for half_row in range(2):
        rows = None
        for part in range(3):
            chosen = [
                jnp.where(slot_hit, split[f][part], 0.0).astype(BF16)
                for f in range(half_row * 4, min(half_row * 4 + 4, 7))
            ]
            if half_row == 1:
                chosen.append(jnp.zeros((slots, count), BF16))
            product = dot_nt(hot_dest[...], jnp.concatenate(chosen, axis=0))
            rows = product if rows is None else rows + product
        out1[:, half_row * LANES : (half_row + 1) * LANES] = rows

    slot_row = slot_ref[...]
    mine = jnp.where(iota((LANES, groups), 0) // MOST == slot_row - me * owned, 1.0, 0.0).astype(BF16)
    limits = jnp.minimum(cap_ref[...], CAP)
    limit_parts = jnp.concatenate([limits // 64, limits % 64], axis=0).astype(F32).astype(BF16)
    limit = dot_nt(limit_parts, mine)
    limit = limit[0:1] * 64.0 + limit[1:2]
    away = order_ref[...]
    source = (((mx // 4 + away[0:1]) & 3) * 4 + ((mx + away[1:2]) & 3)) * ny + (
        ((my // 2 + away[2:3]) & 3) * 2 + ((my + away[3:4]) & 1)
    )
    source = jnp.broadcast_to(source.astype(F32), (LANES, LANES))
    lower = jnp.where(source < source.T, 1.0, 0.0).astype(BF16)
    quarter = (iota((1, LANES), 1) % MOST).astype(F32)

    pl.semaphore_wait(barrier, devices - 1)
    here = (mx, my)
    places = near_first()
    for offset in far_first():
        back = places.index(tuple((size - step) % size for step, size in zip(offset, (4, 4, 4, 2))))
        px, py = peer_at(here, offset)
        pltpu.make_async_remote_copy(
            src_ref=out1.at[pl.ds(px * ny + py, 1)],
            dst_ref=got1.at[pl.ds(back, 1)],
            send_sem=send1,
            recv_sem=recv1,
            device_id=(px, py),
            device_id_type=MESH,
        ).start()
    own = pl.ds(me, 1)
    pltpu.make_async_copy(out1.at[own], got1.at[pl.ds(0, 1)], recv1).start()
    pltpu.make_async_copy(out1.at[own], spare1.at[own], send1).start()

    lane = iota((1, LANES), 1)
    lane8 = iota((8, LANES), 1)
    offset8 = lane8 - iota((8, LANES), 0)

    def row_of(ref, at):
        return jnp.broadcast_to(ref[at : at + 1, :], (8, LANES))

    def column_of(block, at):
        return jnp.broadcast_to(block[:, at : at + 1], (8, LANES))

    def inverse_of(target, there):
        ax, ay, az = [t - h for t, h in zip(target, there)]
        return lax.rsqrt(ax * ax + ay * ay + az * az + SOFTENING_SQ)

    pltpu.make_async_copy(got1, got1, recv1).wait()
    pltpu.make_async_copy(out1, out1, send1).wait()

    first = got1[:, :LANES]
    is_mass = lane < slots
    valid = is_mass & (first > 0.0)
    tally = quad_sum(jnp.where(valid, 1.0, 0.0))
    member_rank = dot(lower, tally.astype(BF16)) + quarter
    keep = valid & (member_rank < limit)
    rows_ref[...] = jnp.where(is_mass & ~keep, 0.0, first).T
    kept_mass = jnp.where(keep, first, 0.0)
    kept_total = quad_sum(jnp.sum(jnp.where(keep, 1.0, 0.0), axis=0, keepdims=True))
    mass_sum = quad_sum(jnp.sum(kept_mass, axis=0, keepdims=True))
    second = got1[:, LANES:]
    stats = [mass_sum * (1.0 / CAP)]
    energy = None
    for axis in range(3):
        speed = second if axis == 0 else pltpu.roll(second, LANES - axis * slots, 1)
        bulk = quad_sum(jnp.sum(kept_mass * speed, axis=0, keepdims=True)) / mass_sum
        stats.append(bulk)
        apart = (speed - bulk) * (speed - bulk)
        energy = apart if energy is None else energy + apart
    motion[...] = jnp.where((lane >= slots) & (lane < 2 * slots), pltpu.roll(0.5 * energy, slots, 1), 0.0)
    rank_or_not = jnp.where(keep, member_rank, -1.0)
    member[...] = jnp.where(
        lane < 3 * slots,
        pltpu.roll(rank_or_not, 2 * slots, 1),
        jnp.broadcast_to(
            jnp.take_along_axis(
                jnp.broadcast_to(kept_total, (8, LANES)), (iota((8, LANES), 1) % owned) * MOST, axis=1
            )[0:1],
            (devices, LANES),
        ),
    )
    spot8 = lane8 % slots
    ones = jnp.ones((2 * LANES, LANES), BF16)

    def conclude(block):
        at = pl.ds(block * 8, 8)
        sums = dot(halves[...], ones)
        pot = jnp.zeros((8, LANES), F32)
        for spot in range(slots):
            pot = jnp.where(spot8 == spot, sums[spot * 8 : spot * 8 + 8], pot)
        both = pot * (-1.0 / CAP) + motion[at, :]
        out2[at, :] = jnp.where(lane8 < 2 * slots, both, member[at, :])

    def pairs_of(block):
        targets = got1[block * 8 : block * 8 + 8, :LANES]
        itself = offset8 == block * 8
        for group in range(owned):
            base = group * MOST
            there = [[row_of(rows_ref, f * slots + base + r) for f in range(4)] for r in range(MOST)]
            totals = []
            for r in range(MOST):
                target = [column_of(targets, f * slots + base + r) for f in range(1, 4)]
                total = None
                for other in range(MOST):
                    value = inverse_of(target, there[other][1:])
                    if r == other:
                        value = jnp.where(itself, 0.0, value)
                    term = value * there[other][0]
                    total = term if total is None else total + term
                totals.append(total)
            for pair in range(0, MOST, 2):
                high, low = parts_of(jnp.concatenate(totals[pair : pair + 2], axis=0), 2)
                lines = pl.ds((group * MOST + pair) * 8, 16)
                halves[lines, :LANES] = high
                halves[lines, LANES:] = low

    def send_block(block):
        for place in range(block * 8 + 7, block * 8 - 1, -1):
            if place:
                pltpu.make_async_remote_copy(
                    src_ref=out2.at[pl.ds(place, 1)],
                    dst_ref=got2.at[own],
                    send_sem=send2,
                    recv_sem=recv2,
                    device_id=peer_at(here, places[place]),
                    device_id_type=MESH,
                ).start()

    last = devices // 8 - 1
    for block in range(last, -1, -1):
        if block < last:
            conclude(block + 1)
        pairs_of(block)
        if block < last:
            send_block(block + 1)
    conclude(0)
    send_block(0)
    pltpu.make_async_copy(out2.at[pl.ds(0, 1)], got2.at[own], recv2).start()
    pltpu.make_async_copy(out2.at[pl.ds(0, 1)], spare2.at[own], send2).start()
    pick = iota((LANES, owned), 0) == iota((LANES, owned), 1) * MOST
    stat_rows = jnp.concatenate(stats + [jnp.zeros((LANES - 4, LANES), F32)], axis=0).T
    for number in range(4):
        cat_ref[number : number + 1, :] = jnp.sum(
            jnp.where(pick, stat_rows[:, number : number + 1], 0.0), axis=0, keepdims=True
        )
    upper = jnp.where(iota((LANES, LANES), 0) < iota((LANES, LANES), 1), 1.0, 0.0).astype(BF16)
    pltpu.make_async_copy(out2, out2, send2).wait()
    pltpu.make_async_copy(got2, got2, recv2).wait()
    answer = got2[...].T
    kept_of = pick_lanes(answer[3 * slots : 3 * slots + owned], slot_row // owned)
    kept_row = jnp.sum(
        jnp.where(iota((owned, groups), 0) == slot_row % owned, kept_of, 0.0), axis=0, keepdims=True
    )
    kept8 = jnp.concatenate(
        [kept_row[:, i * LANES : (i + 1) * LANES] for i in range(half)], axis=0
    )
    kept_parts = parts_of(kept8, 2)
    start8 = dot(kept_parts[0], upper) + dot(kept_parts[1], upper)
    row_total = jnp.sum(kept8, axis=1, keepdims=True)
    running = [jnp.zeros((1, 1), F32)]
    for i in range(half - 1):
        running.append(running[-1] + row_total[i : i + 1])
    start8 = start8 + jnp.concatenate(running, axis=0)
    start = jnp.sum(jnp.where(high_hit, pick_lanes(start8, label_low), 0.0), axis=0, keepdims=True)
    chosen = [
        jnp.sum(
            jnp.where(slot_hit, pick_lanes(answer[v * slots : (v + 1) * slots], dest), 0.0),
            axis=0, keepdims=True,
        )
        for v in range(3)
    ]
    kept = chosen[2] >= 0.0
    index_ref[...] = jnp.where(kept, start + chosen[2], -1.0).astype(I32)
    pot_ref[...] = jnp.where(kept, chosen[0], 0.0)
    bind_ref[...] = jnp.where(kept, chosen[1], 0.0)


def finish(*refs):
    half = len(refs) // 2
    for source, result in zip(refs[:half], refs[half:]):
        result[...] = source[...]


def shards(sizes, positions, velocities, masses, labels, owner_slot, group_cap):
    nx, ny = sizes
    count = masses.shape[0]
    groups = owner_slot.shape[0]
    owned = groups // (nx * ny)
    slots = owned * MOST
    vmem = pl.BlockSpec(memory_space=pltpu.VMEM)
    devices = nx * ny
    wide = lambda width: pltpu.VMEM((devices, width), F32)
    label_row = labels.reshape(1, count)
    slot_row = owner_slot.reshape(1, groups)
    row = lambda dtype: jax.ShapeDtypeStruct((1, count), dtype)
    results = (row(I32), row(F32), row(F32), jax.ShapeDtypeStruct((4, owned), F32))
    inputs = (
        label_row, labels.reshape(count // LANES, LANES), positions, velocities,
        masses.reshape(1, count), owner_slot.reshape(groups // LANES, LANES),
        slot_row, group_cap.reshape(1, groups),
        jnp.array(near_first(), I32).T,
    )
    found = pl.pallas_call(
        functools.partial(kernel, sizes),
        out_shape=results,
        in_specs=[pl.BlockSpec(memory_space=pltpu.HBM)] * 9,
        out_specs=(vmem,) * 4,
        scratch_shapes=[
            *[pltpu.VMEM(array.shape, array.dtype) for array in inputs],
            *[wide(2 * LANES)] * 3,
            *[wide(LANES)] * 3,
            pltpu.VMEM((devices, count), BF16),
            wide(LANES),
            *[wide(LANES)] * 2,
            pltpu.VMEM((slots * 8, 2 * LANES), BF16),
            pltpu.SemaphoreType.DMA((9,)),
            *[pltpu.SemaphoreType.DMA] * 4,
        ],
        compiler_params=pltpu.CompilerParams(
            collective_id=0, has_side_effects=True, vmem_limit_bytes=24 * 2**20
        ),
        name="unbind",
    )(*[pltpu.with_memory_space_constraint(array, pltpu.HBM) for array in inputs])
    index, pot, bind, catalog = pl.pallas_call(
        finish,
        out_shape=results,
        in_specs=[vmem] * 4,
        out_specs=(vmem,) * 4,
        compiler_params=pltpu.CompilerParams(vmem_limit_bytes=2**20),
        name="finish",
    )(*found)
    return (index.reshape(count), pot.reshape(count), bind.reshape(count), catalog)


def solution(mesh):
    sizes = (mesh.shape["gx"], mesh.shape["gy"])
    return jax.shard_map(
        functools.partial(shards, sizes),
        mesh=mesh,
        in_specs=(
            P(None, ("gx", "gy")),
            P(None, ("gx", "gy")),
            P(("gx", "gy")),
            P(("gx", "gy"), None),
            P(),
            P(),
        ),
        out_specs=(P(("gx", "gy")), P(("gx", "gy")), P(("gx", "gy")), P(None, ("gx", "gy"))),
        check_vma=False,
    )
```

```python
import functools

import jax
import jax.numpy as jnp
from jax import lax
from jax.experimental import pallas as pl
from jax.experimental.pallas import tpu as pltpu
from jax.sharding import PartitionSpec as P

CAP = 2048
SOFTENING_SQ = 0.0025
MOST = 4
LANES = 128
MESH = pl.DeviceIdType.MESH
F32, BF16, I32 = jnp.float32, jnp.bfloat16, jnp.int32


def iota(shape, axis):
    return lax.broadcasted_iota(I32, shape, axis)


def onehot(index_row, depth):
    hit = iota((depth, index_row.shape[1]), 0) == index_row
    return jnp.where(hit, 1.0, 0.0).astype(BF16)


def parts_of(value, count):
    found = []
    for step in range(count):
        part = value.astype(BF16)
        found.append(part)
        if step < count - 1:
            value = value - part.astype(F32)
    return found


def pick_lanes(table, index_row):
    found = []
    for at in range(0, index_row.shape[1], LANES):
        index = jnp.broadcast_to(index_row[:, at : at + LANES], (8, LANES))
        found.append(jnp.concatenate([
            jnp.take_along_axis(table[row : row + 8], index, axis=1)
            for row in range(0, table.shape[0], 8)
        ], axis=0))
    return jnp.concatenate(found, axis=1)


def dot(left, right):
    return lax.dot_general(left, right, (((1,), (0,)), ((), ())), preferred_element_type=F32)


def dot_nt(left, right):
    return lax.dot_general(left, right, (((1,), (1,)), ((), ())), preferred_element_type=F32)


def quad_sum(value):
    lane = iota(value.shape, 1)
    for step in (1, 2):
        up = pltpu.roll(value, LANES - step, 1)
        down = pltpu.roll(value, step, 1)
        value = value + jnp.where((lane & step) == 0, up, down)
    return value


def far_first():
    ring = (0, 1, 2, 1)
    offsets = [(dz, dx, dy, dc) for dz in range(4) for dx in range(4) for dy in range(4) for dc in range(2)]
    offsets.sort(key=lambda o: (-(ring[o[0]] + ring[o[1]] + ring[o[2]]), -o[3]))
    return offsets[:-1]


def near_first():
    return [(0, 0, 0, 0)] + far_first()[::-1]


def peer_at(here, offset):
    mx, my = here
    dz, dx, dy, dc = offset
    return (((mx // 4 + dz) % 4) * 4 + (mx + dx) % 4, ((my // 2 + dy) % 4) * 2 + (my + dc) % 2)


def kernel(
    sizes, lab_hbm, lab16_hbm, pos_hbm, vel_hbm, mass_hbm, slot8_hbm, slot_hbm, cap_hbm, order_hbm,
    index_ref, pot_ref, bind_ref, cat_ref,
    lab_ref, lab16_ref, pos_ref, vel_ref, mass_ref, slot8_ref, slot_ref, cap_ref, order_ref,
    out1, spare1, got1, out2, spare2, got2, hot_dest,
    rows_ref, motion, member, halves,
    load_sems, send1, recv1, send2, recv2,
):
    nx, ny = sizes
    devices = nx * ny
    mx, my = lax.axis_index("gx"), lax.axis_index("gy")
    me = mx * ny + my
    count = lab_ref.shape[1]
    groups = slot_ref.shape[1]
    owned = groups // devices
    slots = owned * MOST
    blocks = count // LANES
    half = groups // LANES

    loads = [
        pltpu.make_async_copy(source, place, load_sems.at[number])
        for number, (source, place) in enumerate((
            (lab_hbm, lab_ref), (slot8_hbm, slot8_ref), (lab16_hbm, lab16_ref), (mass_hbm, mass_ref),
            (pos_hbm, pos_ref), (vel_hbm, vel_ref), (slot_hbm, slot_ref), (cap_hbm, cap_ref), (order_hbm, order_ref),
        ))
    ]
    barrier = pltpu.get_barrier_semaphore()
    here = (mx, my)

    for number, offset in enumerate(far_first()):
        if number == 14:
            for load in loads:
                load.start()
        pl.semaphore_signal(barrier, inc=1, device_id=peer_at(here, offset), device_id_type=MESH)
    for load in loads:
        load.wait()

    label = lab_ref[...]
    label_high, label_low = label >> 7, label & 127
    slot8 = slot8_ref[...]
    table = jnp.concatenate([slot8 // owned, slot8 % owned], axis=0).astype(F32).astype(BF16)
    high_hit = iota((half, count), 0) == label_high
    owner = jnp.sum(
        jnp.where(high_hit, pick_lanes(slot8_ref[...], label_low), 0), axis=0, keepdims=True
    )
    dest, local_group = owner // owned, owner % owned

    hot_low = onehot(label_low, LANES)
    high_one = jnp.where(high_hit, 1.0, 0.0)
    none = jnp.zeros((half, LANES), F32)
    prior = jnp.concatenate([
        jnp.concatenate([
            high_one[:, other * LANES : (other + 1) * LANES] if other < block else none
            for other in range(blocks)
        ], axis=1)
        for block in range(blocks)
    ], axis=0).astype(BF16)
    tables = dot_nt(prior, hot_low)
    columns = jnp.concatenate(
        [lab16_ref[...], jnp.zeros((LANES - blocks, LANES), I32)], axis=0
    ).astype(F32).T.astype(I32)
    triangle = jnp.where(iota((LANES, LANES), 0) < iota((LANES, LANES), 1), 1.0, 0.0)
    ranks = []
    for block in range(blocks):
        lanes = slice(block * LANES, (block + 1) * LANES)
        column = jnp.broadcast_to(columns[:, block : block + 1], (LANES, LANES))
        within = jnp.where(column == label[:, lanes], triangle, 0.0)
        before = jnp.where(
            high_hit[:, lanes], pick_lanes(tables[block * half : (block + 1) * half], label_low[:, lanes]), 0.0
        )
        within = jnp.sum(within.reshape(LANES // half, half, LANES), axis=0)
        ranks.append(jnp.sum(before + within, axis=0, keepdims=True))
    rank = jnp.concatenate(ranks, axis=1).astype(I32)
    slot = local_group * MOST + rank

    hot_dest[...] = onehot(dest, devices)
    slot_hit = iota((slots, count), 0) == slot
    fields = [mass_ref[...], pos_ref[0:1, :], pos_ref[1:2, :], pos_ref[2:3, :],
              vel_ref[0:1, :], vel_ref[1:2, :], vel_ref[2:3, :]]
    split = [[part.astype(F32) for part in parts_of(field, 3)] for field in fields]
    outgoing = None
    for part in range(3):
        chosen = [jnp.where(slot_hit, split[f][part], 0.0).astype(BF16) for f in range(7)]
        chosen.append(jnp.zeros((slots, count), BF16))
        product = dot_nt(hot_dest[...], jnp.concatenate(chosen, axis=0))
        outgoing = product if outgoing is None else outgoing + product
    out1[...] = outgoing

    slot_row = slot_ref[...]
    mine = jnp.where(iota((LANES, groups), 0) // MOST == slot_row - me * owned, 1.0, 0.0).astype(BF16)
    limits = jnp.minimum(cap_ref[...], CAP)
    limit_parts = jnp.concatenate([limits // 64, limits % 64], axis=0).astype(F32).astype(BF16)
    limit = dot_nt(limit_parts, mine)
    limit = limit[0:1] * 64.0 + limit[1:2]
    away = order_ref[...]
    source = (((mx // 4 + away[0:1]) & 3) * 4 + ((mx + away[1:2]) & 3)) * ny + (
        ((my // 2 + away[2:3]) & 3) * 2 + ((my + away[3:4]) & 1)
    )
    source = jnp.broadcast_to(source.astype(F32), (LANES, LANES))
    lower = jnp.where(source < source.T, 1.0, 0.0).astype(BF16)
    quad = jnp.where(
        iota((LANES, LANES), 0) // MOST == iota((LANES, LANES), 1) // MOST, 1.0, 0.0
    ).astype(BF16)
    quarter = (iota((1, LANES), 1) % MOST).astype(F32)

    pl.semaphore_wait(barrier, devices - 1)
    here = (mx, my)
    places = near_first()
    for offset in far_first():
        back = places.index(tuple((size - step) % size for step, size in zip(offset, (4, 4, 4, 2))))
        px, py = peer_at(here, offset)
        pltpu.make_async_remote_copy(
            src_ref=out1.at[pl.ds(px * ny + py, 1)],
            dst_ref=got1.at[pl.ds(back, 1)],
            send_sem=send1,
            recv_sem=recv1,
            device_id=(px, py),
            device_id_type=MESH,
        ).start()
    own = pl.ds(me, 1)
    pltpu.make_async_copy(out1.at[own], got1.at[pl.ds(0, 1)], recv1).start()
    pltpu.make_async_copy(out1.at[own], spare1.at[own], send1).start()

    lane = iota((1, LANES), 1)
    lane8 = iota((8, LANES), 1)
    offset8 = lane8 - iota((8, LANES), 0)

    def row_of(ref, at):
        return jnp.broadcast_to(ref[at : at + 1, :], (8, LANES))

    def column_of(block, at):
        return jnp.broadcast_to(block[:, at : at + 1], (8, LANES))

    def inverse_of(target, there):
        ax, ay, az = [t - h for t, h in zip(target, there)]
        return lax.rsqrt(ax * ax + ay * ay + az * az + SOFTENING_SQ)

    pltpu.make_async_copy(got1, got1, recv1).wait()
    pltpu.make_async_copy(out1, out1, send1).wait()

    first = got1[:, :LANES]
    is_mass = lane < slots
    valid = is_mass & (first > 0.0)
    earlier = dot(lower, jnp.where(valid, 1.0, 0.0).astype(BF16))
    member_rank = dot(earlier.astype(BF16), quad) + quarter
    keep = valid & (member_rank < limit)
    kept_mass = jnp.where(keep, first, 0.0)
    rows_ref[slots:] = first.T[slots:]
    rows_ref[:slots] = kept_mass.T[:slots]
    kept_total = quad_sum(jnp.sum(jnp.where(keep, 1.0, 0.0), axis=0, keepdims=True))
    mass_sum = quad_sum(jnp.sum(kept_mass, axis=0, keepdims=True))
    second = got1[:, LANES:]
    stats = [mass_sum * (1.0 / CAP)]
    energy = None
    for axis in range(3):
        speed = second if axis == 0 else pltpu.roll(second, LANES - axis * slots, 1)
        bulk = quad_sum(jnp.sum(kept_mass * speed, axis=0, keepdims=True)) / mass_sum
        stats.append(bulk)
        apart = (speed - bulk) * (speed - bulk)
        energy = apart if energy is None else energy + apart
    motion[...] = jnp.where(lane < slots, 0.5 * energy, 0.0)
    rank_or_not = jnp.where(keep, member_rank, -1.0)
    member[...] = jnp.where(
        lane < 3 * slots,
        pltpu.roll(rank_or_not, 2 * slots, 1),
        jnp.broadcast_to(
            jnp.take_along_axis(
                jnp.broadcast_to(kept_total, (8, LANES)), (iota((8, LANES), 1) % owned) * MOST, axis=1
            )[0:1],
            (devices, LANES),
        ),
    )
    spot8 = lane8 % slots
    ones = jnp.ones((2 * LANES, LANES), BF16)

    def conclude(block):
        at = pl.ds(block * 8, 8)
        sums = dot(halves[...], ones)
        pot = jnp.zeros((8, LANES), F32)
        for spot in range(slots):
            pot = jnp.where(spot8 == spot, sums[spot * 8 : spot * 8 + 8], pot)
        both = pot * (-1.0 / CAP) + motion[at, :]
        out2[at, :] = jnp.where(lane8 < 2 * slots, both, member[at, :])

    def pairs_of(block):
        targets = got1[block * 8 : block * 8 + 8, :LANES]
        itself = offset8 == block * 8
        for group in range(owned):
            base = group * MOST
            there = [[row_of(rows_ref, f * slots + base + r) for f in range(4)] for r in range(MOST)]
            totals = []
            for r in range(MOST):
                target = [column_of(targets, f * slots + base + r) for f in range(1, 4)]
                total = None
                for other in range(MOST):
                    value = inverse_of(target, there[other][1:])
                    if r == other:
                        value = jnp.where(itself, 0.0, value)
                    term = value * there[other][0]
                    total = term if total is None else total + term
                totals.append(total)
            for pair in range(0, MOST, 2):
                high, low = parts_of(jnp.concatenate(totals[pair : pair + 2], axis=0), 2)
                lines = pl.ds((group * MOST + pair) * 8, 16)
                halves[lines, :LANES] = high
                halves[lines, LANES:] = low

    def send_block(block):
        for place in range(block * 8 + 7, block * 8 - 1, -1):
            if place:
                pltpu.make_async_remote_copy(
                    src_ref=out2.at[pl.ds(place, 1)],
                    dst_ref=got2.at[own],
                    send_sem=send2,
                    recv_sem=recv2,
                    device_id=peer_at(here, places[place]),
                    device_id_type=MESH,
                ).start()

    last = devices // 8 - 1
    gone = []
    for block in range(last, -1, -1):
        if block < last - 1:
            conclude(block + 1)
            gone.append(block + 1)
        pairs_of(block)
        if block == last:
            conclude(block)
            gone.append(block)
        if block >= last - 2 or block <= 5 or block % 2 == 0:
            for ready in gone:
                send_block(ready)
            gone = []
    conclude(0)
    send_block(0)
    pltpu.make_async_copy(out2.at[pl.ds(0, 1)], got2.at[own], recv2).start()
    pltpu.make_async_copy(out2.at[pl.ds(0, 1)], spare2.at[own], send2).start()
    pick = iota((LANES, owned), 0) == iota((LANES, owned), 1) * MOST
    stat_rows = jnp.concatenate(stats + [jnp.zeros((LANES - 4, LANES), F32)], axis=0).T
    for number in range(4):
        cat_ref[number : number + 1, :] = jnp.sum(
            jnp.where(pick, stat_rows[:, number : number + 1], 0.0), axis=0, keepdims=True
        )
    upper = jnp.where(iota((LANES, LANES), 0) < iota((LANES, LANES), 1), 1.0, 0.0).astype(BF16)
    pltpu.make_async_copy(out2, out2, send2).wait()
    pltpu.make_async_copy(got2, got2, recv2).wait()
    answer = got2[...].T
    kept_of = pick_lanes(answer[3 * slots : 3 * slots + owned], slot_row // owned)
    kept_row = jnp.sum(
        jnp.where(iota((owned, groups), 0) == slot_row % owned, kept_of, 0.0), axis=0, keepdims=True
    )
    kept8 = jnp.concatenate(
        [kept_row[:, i * LANES : (i + 1) * LANES] for i in range(half)], axis=0
    )
    kept_parts = parts_of(kept8, 2)
    start8 = dot(kept_parts[0], upper) + dot(kept_parts[1], upper)
    ahead = jnp.broadcast_to(jnp.sum(kept8, axis=1, keepdims=True), (half, LANES))
    row8 = iota((half, LANES), 0)
    ahead = jnp.where(row8 >= 1, pltpu.roll(ahead, 1, 0), 0.0)
    for step in (1, 2, 4):
        ahead = ahead + jnp.where(row8 >= step, pltpu.roll(ahead, step, 0), 0.0)
    start8 = start8 + ahead
    start = jnp.sum(jnp.where(high_hit, pick_lanes(start8, label_low), 0.0), axis=0, keepdims=True)
    chosen = [
        jnp.sum(
            jnp.where(slot_hit, pick_lanes(answer[v * slots : (v + 1) * slots], dest), 0.0),
            axis=0, keepdims=True,
        )
        for v in range(3)
    ]
    kept = chosen[2] >= 0.0
    index_ref[...] = jnp.where(kept, start + chosen[2], -1.0).astype(I32)
    pot_ref[...] = jnp.where(kept, chosen[1], 0.0)
    bind_ref[...] = jnp.where(kept, chosen[0], 0.0)


def finish(*refs):
    half = len(refs) // 2
    for source, result in zip(refs[:half], refs[half:]):
        result[...] = source[...]


def shards(sizes, positions, velocities, masses, labels, owner_slot, group_cap):
    nx, ny = sizes
    count = masses.shape[0]
    groups = owner_slot.shape[0]
    owned = groups // (nx * ny)
    slots = owned * MOST
    vmem = pl.BlockSpec(memory_space=pltpu.VMEM)
    devices = nx * ny
    wide = lambda width: pltpu.VMEM((devices, width), F32)
    label_row = labels.reshape(1, count)
    slot_row = owner_slot.reshape(1, groups)
    row = lambda dtype: jax.ShapeDtypeStruct((1, count), dtype)
    results = (row(I32), row(F32), row(F32), jax.ShapeDtypeStruct((4, owned), F32))
    inputs = (
        label_row, labels.reshape(count // LANES, LANES), positions, velocities,
        masses.reshape(1, count), owner_slot.reshape(groups // LANES, LANES),
        slot_row, group_cap.reshape(1, groups),
        jnp.array(near_first(), I32).T,
    )
    found = pl.pallas_call(
        functools.partial(kernel, sizes),
        out_shape=results,
        in_specs=[pl.BlockSpec(memory_space=pltpu.HBM)] * 9,
        out_specs=(vmem,) * 4,
        scratch_shapes=[
            *[pltpu.VMEM(array.shape, array.dtype) for array in inputs],
            *[wide(2 * LANES)] * 3,
            *[wide(LANES)] * 3,
            pltpu.VMEM((devices, count), BF16),
            wide(LANES),
            *[wide(LANES)] * 2,
            pltpu.VMEM((slots * 8, 2 * LANES), BF16),
            pltpu.SemaphoreType.DMA((9,)),
            *[pltpu.SemaphoreType.DMA] * 4,
        ],
        compiler_params=pltpu.CompilerParams(
            collective_id=0, has_side_effects=True, vmem_limit_bytes=24 * 2**20
        ),
        name="unbind",
    )(*[pltpu.with_memory_space_constraint(array, pltpu.HBM) for array in inputs])
    index, pot, bind, catalog = pl.pallas_call(
        finish,
        out_shape=results,
        in_specs=[vmem] * 4,
        out_specs=(vmem,) * 4,
        compiler_params=pltpu.CompilerParams(vmem_limit_bytes=2**20),
        name="finish",
    )(*found)
    return (index.reshape(count), pot.reshape(count), bind.reshape(count), catalog)


def solution(mesh):
    sizes = (mesh.shape["gx"], mesh.shape["gy"])
    return jax.shard_map(
        functools.partial(shards, sizes),
        mesh=mesh,
        in_specs=(
            P(None, ("gx", "gy")),
            P(None, ("gx", "gy")),
            P(("gx", "gy")),
            P(("gx", "gy"), None),
            P(),
            P(),
        ),
        out_specs=(P(("gx", "gy")), P(("gx", "gy")), P(("gx", "gy")), P(None, ("gx", "gy"))),
        check_vma=False,
    )
```

```python
import functools

import jax
import jax.numpy as jnp
from jax import lax
from jax.experimental import pallas as pl
from jax.experimental.pallas import tpu as pltpu
from jax.sharding import PartitionSpec as P

CAP = 2048
SOFTENING_SQ = 0.0025
MOST = 4
LANES = 128
MESH = pl.DeviceIdType.MESH
F32, BF16, I32 = jnp.float32, jnp.bfloat16, jnp.int32


def iota(shape, axis):
    return lax.broadcasted_iota(I32, shape, axis)


def onehot(index_row, depth):
    hit = iota((depth, index_row.shape[1]), 0) == index_row
    return jnp.where(hit, 1.0, 0.0).astype(BF16)


def parts_of(value, count):
    found = []
    for step in range(count):
        part = value.astype(BF16)
        found.append(part)
        if step < count - 1:
            value = value - part.astype(F32)
    return found


def pick_lanes(table, index_row):
    found = []
    for at in range(0, index_row.shape[1], LANES):
        index = jnp.broadcast_to(index_row[:, at : at + LANES], (8, LANES))
        found.append(jnp.concatenate([
            jnp.take_along_axis(table[row : row + 8], index, axis=1)
            for row in range(0, table.shape[0], 8)
        ], axis=0))
    return jnp.concatenate(found, axis=1)


def dot(left, right):
    return lax.dot_general(left, right, (((1,), (0,)), ((), ())), preferred_element_type=F32)


def dot_nt(left, right):
    return lax.dot_general(left, right, (((1,), (1,)), ((), ())), preferred_element_type=F32)


def quad_sum(value):
    lane = iota(value.shape, 1)
    for step in (1, 2):
        up = pltpu.roll(value, LANES - step, 1)
        down = pltpu.roll(value, step, 1)
        value = value + jnp.where((lane & step) == 0, up, down)
    return value


def far_first():
    ring = (0, 1, 2, 1)
    offsets = [(dz, dx, dy, dc) for dz in range(4) for dx in range(4) for dy in range(4) for dc in range(2)]
    offsets.sort(key=lambda o: (-(ring[o[0]] + ring[o[1]] + ring[o[2]]), -o[3]))
    return offsets[:-1]


def near_first():
    return [(0, 0, 0, 0)] + far_first()[::-1]


def peer_at(here, offset):
    mx, my = here
    dz, dx, dy, dc = offset
    return (((mx // 4 + dz) % 4) * 4 + (mx + dx) % 4, ((my // 2 + dy) % 4) * 2 + (my + dc) % 2)


def kernel(
    sizes, lab_hbm, lab16_hbm, pos_hbm, vel_hbm, mass_hbm, slot8_hbm, slot_hbm, cap_hbm, order_hbm,
    index_ref, pot_ref, bind_ref, cat_ref,
    lab_ref, lab16_ref, pos_ref, vel_ref, mass_ref, slot8_ref, slot_ref, cap_ref, order_ref,
    out1, spare1, got1, out2, spare2, got2, hot_dest,
    rows_ref, motion, member, halves,
    load_sems, send1, recv1, send2, recv2,
):
    nx, ny = sizes
    devices = nx * ny
    mx, my = lax.axis_index("gx"), lax.axis_index("gy")
    me = mx * ny + my
    count = lab_ref.shape[1]
    groups = slot_ref.shape[1]
    owned = groups // devices
    slots = owned * MOST
    blocks = count // LANES
    half = groups // LANES

    loads = [
        pltpu.make_async_copy(source, place, load_sems.at[number])
        for number, (source, place) in enumerate((
            (lab_hbm, lab_ref), (slot8_hbm, slot8_ref), (lab16_hbm, lab16_ref), (mass_hbm, mass_ref),
            (pos_hbm, pos_ref), (vel_hbm, vel_ref), (slot_hbm, slot_ref), (cap_hbm, cap_ref), (order_hbm, order_ref),
        ))
    ]
    barrier = pltpu.get_barrier_semaphore()
    here = (mx, my)

    for number, offset in enumerate(far_first()):
        if number == 14:
            for load in loads:
                load.start()
        pl.semaphore_signal(barrier, inc=1, device_id=peer_at(here, offset), device_id_type=MESH)
    for load in loads:
        load.wait()

    label = lab_ref[...]
    label_high, label_low = label >> 7, label & 127
    slot8 = slot8_ref[...]
    table = jnp.concatenate([slot8 // owned, slot8 % owned], axis=0).astype(F32).astype(BF16)
    high_hit = iota((half, count), 0) == label_high
    owner = jnp.sum(
        jnp.where(high_hit, pick_lanes(slot8_ref[...], label_low), 0), axis=0, keepdims=True
    )
    dest, local_group = owner // owned, owner % owned

    hot_low = onehot(label_low, LANES)
    high_one = jnp.where(high_hit, 1.0, 0.0)
    none = jnp.zeros((half, LANES), F32)
    prior = jnp.concatenate([
        jnp.concatenate([
            high_one[:, other * LANES : (other + 1) * LANES] if other < block else none
            for other in range(blocks)
        ], axis=1)
        for block in range(blocks)
    ], axis=0).astype(BF16)
    tables = dot_nt(prior, hot_low)
    columns = jnp.concatenate(
        [lab16_ref[...], jnp.zeros((LANES - blocks, LANES), I32)], axis=0
    ).astype(F32).T.astype(I32)
    triangle = jnp.where(iota((LANES, LANES), 0) < iota((LANES, LANES), 1), 1.0, 0.0)
    ranks = []
    for block in range(blocks):
        lanes = slice(block * LANES, (block + 1) * LANES)
        column = jnp.broadcast_to(columns[:, block : block + 1], (LANES, LANES))
        within = jnp.where(column == label[:, lanes], triangle, 0.0)
        before = jnp.where(
            high_hit[:, lanes], pick_lanes(tables[block * half : (block + 1) * half], label_low[:, lanes]), 0.0
        )
        within = jnp.sum(within.reshape(LANES // half, half, LANES), axis=0)
        ranks.append(jnp.sum(before + within, axis=0, keepdims=True))
    rank = jnp.concatenate(ranks, axis=1).astype(I32)
    slot = local_group * MOST + rank

    hot_dest[...] = onehot(dest, devices)
    slot_hit = iota((slots, count), 0) == slot
    fields = [mass_ref[...], pos_ref[0:1, :], pos_ref[1:2, :], pos_ref[2:3, :],
              vel_ref[0:1, :], vel_ref[1:2, :], vel_ref[2:3, :]]
    split = [[part.astype(F32) for part in parts_of(field, 3)] for field in fields]
    outgoing = None
    for part in range(3):
        chosen = [jnp.where(slot_hit, split[f][part], 0.0).astype(BF16) for f in range(7)]
        chosen.append(jnp.zeros((slots, count), BF16))
        product = dot_nt(hot_dest[...], jnp.concatenate(chosen, axis=0))
        outgoing = product if outgoing is None else outgoing + product
    out1[...] = outgoing

    slot_row = slot_ref[...]
    mine = jnp.where(iota((LANES, groups), 0) // MOST == slot_row - me * owned, 1.0, 0.0).astype(BF16)
    limits = jnp.minimum(cap_ref[...], CAP)
    limit_parts = jnp.concatenate([limits // 64, limits % 64], axis=0).astype(F32).astype(BF16)
    limit = dot_nt(limit_parts, mine)
    limit = limit[0:1] * 64.0 + limit[1:2]
    away = order_ref[...]
    source = (((mx // 4 + away[0:1]) & 3) * 4 + ((mx + away[1:2]) & 3)) * ny + (
        ((my // 2 + away[2:3]) & 3) * 2 + ((my + away[3:4]) & 1)
    )
    source = jnp.broadcast_to(source.astype(F32), (LANES, LANES))
    lower = jnp.where(source < source.T, 1.0, 0.0).astype(BF16)
    quad = jnp.where(
        iota((LANES, LANES), 0) // MOST == iota((LANES, LANES), 1) // MOST, 1.0, 0.0
    ).astype(BF16)
    quarter = (iota((1, LANES), 1) % MOST).astype(F32)

    pl.semaphore_wait(barrier, devices - 1)
    here = (mx, my)
    places = near_first()
    for offset in far_first():
        back = places.index(tuple((size - step) % size for step, size in zip(offset, (4, 4, 4, 2))))
        px, py = peer_at(here, offset)
        pltpu.make_async_remote_copy(
            src_ref=out1.at[pl.ds(px * ny + py, 1)],
            dst_ref=got1.at[pl.ds(back, 1)],
            send_sem=send1,
            recv_sem=recv1,
            device_id=(px, py),
            device_id_type=MESH,
        ).start()
    own = pl.ds(me, 1)
    pltpu.make_async_copy(out1.at[own], got1.at[pl.ds(0, 1)], recv1).start()
    pltpu.make_async_copy(out1.at[own], spare1.at[own], send1).start()

    lane = iota((1, LANES), 1)
    lane8 = iota((8, LANES), 1)
    offset8 = lane8 - iota((8, LANES), 0)

    def row_of(ref, at):
        return jnp.broadcast_to(ref[at : at + 1, :], (8, LANES))

    def column_of(block, at):
        return jnp.broadcast_to(block[:, at : at + 1], (8, LANES))

    def inverse_of(target, there):
        ax, ay, az = [t - h for t, h in zip(target, there)]
        return lax.rsqrt(ax * ax + ay * ay + az * az + SOFTENING_SQ)

    pltpu.make_async_copy(got1, got1, recv1).wait()

    first = got1[:, :LANES]
    is_mass = lane < slots
    valid = is_mass & (first > 0.0)
    earlier = dot(lower, jnp.where(valid, 1.0, 0.0).astype(BF16))
    member_rank = dot(earlier.astype(BF16), quad) + quarter
    keep = valid & (member_rank < limit)
    kept_mass = jnp.where(keep, first, 0.0)
    rows_ref[slots:] = first.T[slots:]
    rows_ref[:slots] = kept_mass.T[:slots]
    kept_total = quad_sum(jnp.sum(jnp.where(keep, 1.0, 0.0), axis=0, keepdims=True))
    mass_sum = quad_sum(jnp.sum(kept_mass, axis=0, keepdims=True))
    second = got1[:, LANES:]
    stats = [mass_sum * (1.0 / CAP)]
    energy = None
    for axis in range(3):
        speed = second if axis == 0 else pltpu.roll(second, LANES - axis * slots, 1)
        bulk = quad_sum(jnp.sum(kept_mass * speed, axis=0, keepdims=True)) / mass_sum
        stats.append(bulk)
        apart = (speed - bulk) * (speed - bulk)
        energy = apart if energy is None else energy + apart
    motion[...] = jnp.where(lane < slots, 0.5 * energy, 0.0)
    rank_or_not = jnp.where(keep, member_rank, -1.0)
    member[...] = jnp.where(
        lane < 3 * slots,
        pltpu.roll(rank_or_not, 2 * slots, 1),
        jnp.broadcast_to(
            jnp.take_along_axis(
                jnp.broadcast_to(kept_total, (8, LANES)), (iota((8, LANES), 1) % owned) * MOST, axis=1
            )[0:1],
            (devices, LANES),
        ),
    )
    spot8 = lane8 % slots
    ones = jnp.ones((2 * LANES, LANES), BF16)

    def conclude(block):
        at = pl.ds(block * 8, 8)
        sums = dot(halves[...], ones)
        pot = jnp.zeros((8, LANES), F32)
        for spot in range(slots):
            pot = jnp.where(spot8 == spot, sums[spot * 8 : spot * 8 + 8], pot)
        both = pot * (-1.0 / CAP) + motion[at, :]
        out2[at, :] = jnp.where(lane8 < 2 * slots, both, member[at, :])

    def pairs_of(block):
        targets = got1[block * 8 : block * 8 + 8, :LANES]
        itself = offset8 == block * 8
        for group in range(owned):
            base = group * MOST
            there = [[row_of(rows_ref, f * slots + base + r) for f in range(4)] for r in range(MOST)]
            totals = []
            for r in range(MOST):
                target = [column_of(targets, f * slots + base + r) for f in range(1, 4)]
                total = None
                for other in range(MOST):
                    value = inverse_of(target, there[other][1:])
                    if r == other:
                        value = jnp.where(itself, 0.0, value)
                    term = value * there[other][0]
                    total = term if total is None else total + term
                totals.append(total)
            for pair in range(0, MOST, 2):
                high, low = parts_of(jnp.concatenate(totals[pair : pair + 2], axis=0), 2)
                lines = pl.ds((group * MOST + pair) * 8, 16)
                halves[lines, :LANES] = high
                halves[lines, LANES:] = low

    def send_block(block):
        for place in range(block * 8 + 7, block * 8 - 1, -1):
            if place:
                pltpu.make_async_remote_copy(
                    src_ref=out2.at[pl.ds(place, 1)],
                    dst_ref=got2.at[own],
                    send_sem=send2,
                    recv_sem=recv2,
                    device_id=peer_at(here, places[place]),
                    device_id_type=MESH,
                ).start()

    last = devices // 8 - 1
    gone = []
    for block in range(last, -1, -1):
        if block < last - 1:
            conclude(block + 1)
            gone.append(block + 1)
        pairs_of(block)
        if block == last:
            conclude(block)
            gone.append(block)
        if block >= last - 2 or block <= 5 or block % 2 == 0:
            for ready in gone:
                send_block(ready)
            gone = []
    conclude(0)
    send_block(0)
    pltpu.make_async_copy(out2.at[pl.ds(0, 1)], got2.at[own], recv2).start()
    pltpu.make_async_copy(out2.at[pl.ds(0, 1)], spare2.at[own], send2).start()
    pick = iota((LANES, owned), 0) == iota((LANES, owned), 1) * MOST
    stat_rows = jnp.concatenate(stats + [jnp.zeros((LANES - 4, LANES), F32)], axis=0).T
    for number in range(4):
        cat_ref[number : number + 1, :] = jnp.sum(
            jnp.where(pick, stat_rows[:, number : number + 1], 0.0), axis=0, keepdims=True
        )
    upper = jnp.where(iota((LANES, LANES), 0) < iota((LANES, LANES), 1), 1.0, 0.0).astype(BF16)
    pltpu.make_async_copy(got2, got2, recv2).wait()
    answer = got2[...].T
    kept_of = pick_lanes(answer[3 * slots : 3 * slots + owned], slot_row // owned)
    kept_row = jnp.sum(
        jnp.where(iota((owned, groups), 0) == slot_row % owned, kept_of, 0.0), axis=0, keepdims=True
    )
    kept8 = jnp.concatenate(
        [kept_row[:, i * LANES : (i + 1) * LANES] for i in range(half)], axis=0
    )
    kept_parts = parts_of(kept8, 2)
    start8 = dot(kept_parts[0], upper) + dot(kept_parts[1], upper)
    ahead = jnp.broadcast_to(jnp.sum(kept8, axis=1, keepdims=True), (half, LANES))
    row8 = iota((half, LANES), 0)
    ahead = jnp.where(row8 >= 1, pltpu.roll(ahead, 1, 0), 0.0)
    for step in (1, 2, 4):
        ahead = ahead + jnp.where(row8 >= step, pltpu.roll(ahead, step, 0), 0.0)
    start8 = start8 + ahead
    start = jnp.sum(jnp.where(high_hit, pick_lanes(start8, label_low), 0.0), axis=0, keepdims=True)
    chosen = [
        jnp.sum(
            jnp.where(slot_hit, pick_lanes(answer[v * slots : (v + 1) * slots], dest), 0.0),
            axis=0, keepdims=True,
        )
        for v in range(3)
    ]
    kept = chosen[2] >= 0.0
    index_ref[...] = jnp.where(kept, start + chosen[2], -1.0).astype(I32)
    pot_ref[...] = jnp.where(kept, chosen[1], 0.0)
    bind_ref[...] = jnp.where(kept, chosen[0], 0.0)
    pltpu.make_async_copy(out1, out1, send1).wait()
    pltpu.make_async_copy(out2, out2, send2).wait()


def finish(*refs):
    sems = refs[-1]
    half = (len(refs) - 1) // 2
    copies = [
        pltpu.make_async_copy(source, result, sems.at[number])
        for number, (source, result) in enumerate(zip(refs[:half], refs[half:-1]))
    ]
    for copy in copies:
        copy.start()
    for copy in copies:
        copy.wait()


def shards(sizes, positions, velocities, masses, labels, owner_slot, group_cap):
    nx, ny = sizes
    count = masses.shape[0]
    groups = owner_slot.shape[0]
    owned = groups // (nx * ny)
    slots = owned * MOST
    vmem = pl.BlockSpec(memory_space=pltpu.VMEM)
    devices = nx * ny
    wide = lambda width: pltpu.VMEM((devices, width), F32)
    label_row = labels.reshape(1, count)
    slot_row = owner_slot.reshape(1, groups)
    row = lambda dtype: jax.ShapeDtypeStruct((1, count), dtype)
    results = (row(I32), row(F32), row(F32), jax.ShapeDtypeStruct((4, owned), F32))
    inputs = (
        label_row, labels.reshape(count // LANES, LANES), positions, velocities,
        masses.reshape(1, count), owner_slot.reshape(groups // LANES, LANES),
        slot_row, group_cap.reshape(1, groups),
        jnp.array(near_first(), I32).T,
    )
    found = pl.pallas_call(
        functools.partial(kernel, sizes),
        out_shape=results,
        in_specs=[pl.BlockSpec(memory_space=pltpu.HBM)] * 9,
        out_specs=(vmem,) * 4,
        scratch_shapes=[
            *[pltpu.VMEM(array.shape, array.dtype) for array in inputs],
            *[wide(2 * LANES)] * 3,
            *[wide(LANES)] * 3,
            pltpu.VMEM((devices, count), BF16),
            wide(LANES),
            *[wide(LANES)] * 2,
            pltpu.VMEM((slots * 8, 2 * LANES), BF16),
            pltpu.SemaphoreType.DMA((9,)),
            *[pltpu.SemaphoreType.DMA] * 4,
        ],
        compiler_params=pltpu.CompilerParams(
            collective_id=0, has_side_effects=True, vmem_limit_bytes=24 * 2**20
        ),
        name="unbind",
    )(*[pltpu.with_memory_space_constraint(array, pltpu.HBM) for array in inputs])
    index, pot, bind, catalog = pl.pallas_call(
        finish,
        out_shape=results,
        in_specs=[vmem] * 4,
        out_specs=(pl.BlockSpec(memory_space=pltpu.HBM),) * 4,
        scratch_shapes=[pltpu.SemaphoreType.DMA((4,))],
        compiler_params=pltpu.CompilerParams(vmem_limit_bytes=2**20),
        name="finish",
    )(*found)
    return (index.reshape(count), pot.reshape(count), bind.reshape(count), catalog)


def solution(mesh):
    sizes = (mesh.shape["gx"], mesh.shape["gy"])
    return jax.shard_map(
        functools.partial(shards, sizes),
        mesh=mesh,
        in_specs=(
            P(None, ("gx", "gy")),
            P(None, ("gx", "gy")),
            P(("gx", "gy")),
            P(("gx", "gy"), None),
            P(),
            P(),
        ),
        out_specs=(P(("gx", "gy")), P(("gx", "gy")), P(("gx", "gy")), P(None, ("gx", "gy"))),
        check_vma=False,
    )
```

```python
import functools

import jax
import jax.numpy as jnp
from jax import lax
from jax.experimental import pallas as pl
from jax.experimental.pallas import tpu as pltpu
from jax.sharding import PartitionSpec as P

CAP = 2048
SOFTENING_SQ = 0.0025
MOST = 4
LANES = 128
MESH = pl.DeviceIdType.MESH
F32, BF16, I32 = jnp.float32, jnp.bfloat16, jnp.int32


def iota(shape, axis):
    return lax.broadcasted_iota(I32, shape, axis)


def onehot(index_row, depth):
    hit = iota((depth, index_row.shape[1]), 0) == index_row
    return jnp.where(hit, 1.0, 0.0).astype(BF16)


def parts_of(value, count):
    found = []
    for step in range(count):
        part = value.astype(BF16)
        found.append(part)
        if step < count - 1:
            value = value - part.astype(F32)
    return found


def pick_lanes(table, index_row):
    found = []
    for at in range(0, index_row.shape[1], LANES):
        index = jnp.broadcast_to(index_row[:, at : at + LANES], (8, LANES))
        found.append(jnp.concatenate([
            jnp.take_along_axis(table[row : row + 8], index, axis=1)
            for row in range(0, table.shape[0], 8)
        ], axis=0))
    return jnp.concatenate(found, axis=1)


def dot(left, right):
    return lax.dot_general(left, right, (((1,), (0,)), ((), ())), preferred_element_type=F32)


def dot_nt(left, right):
    return lax.dot_general(left, right, (((1,), (1,)), ((), ())), preferred_element_type=F32)


def quad_sum(value):
    lane = iota(value.shape, 1)
    for step in (1, 2):
        up = pltpu.roll(value, LANES - step, 1)
        down = pltpu.roll(value, step, 1)
        value = value + jnp.where((lane & step) == 0, up, down)
    return value


def far_first():
    ring = (0, 1, 2, 1)
    offsets = [(dz, dx, dy, dc) for dz in range(4) for dx in range(4) for dy in range(4) for dc in range(2)]
    offsets.sort(key=lambda o: (-(ring[o[0]] + ring[o[1]] + ring[o[2]]), -o[3]))
    return offsets[:-1]


def near_first():
    return [(0, 0, 0, 0)] + far_first()[::-1]


def peer_at(here, offset):
    mx, my = here
    dz, dx, dy, dc = offset
    return (((mx // 4 + dz) % 4) * 4 + (mx + dx) % 4, ((my // 2 + dy) % 4) * 2 + (my + dc) % 2)


def kernel(
    sizes, lab_hbm, lab16_hbm, pos_hbm, vel_hbm, mass_hbm, slot8_hbm, slot_hbm, cap_hbm, order_hbm,
    index_ref, pot_ref, bind_ref, cat_ref,
    lab_ref, lab16_ref, pos_ref, vel_ref, mass_ref, slot8_ref, slot_ref, cap_ref, order_ref,
    out1, spare1, got1, out2, spare2, got2, hot_dest,
    rows_ref, motion, member, halves,
    load_sems, send1, recv1, send2, recv2,
):
    nx, ny = sizes
    devices = nx * ny
    mx, my = lax.axis_index("gx"), lax.axis_index("gy")
    me = mx * ny + my
    count = lab_ref.shape[1]
    groups = slot_ref.shape[1]
    owned = groups // devices
    slots = owned * MOST
    blocks = count // LANES
    half = groups // LANES

    loads = [
        pltpu.make_async_copy(source, place, load_sems.at[number])
        for number, (source, place) in enumerate((
            (lab_hbm, lab_ref), (slot8_hbm, slot8_ref), (lab16_hbm, lab16_ref), (mass_hbm, mass_ref),
            (pos_hbm, pos_ref), (vel_hbm, vel_ref), (slot_hbm, slot_ref), (cap_hbm, cap_ref), (order_hbm, order_ref),
        ))
    ]
    barrier = pltpu.get_barrier_semaphore()
    here = (mx, my)

    for number, offset in enumerate(far_first()):
        if number == 14:
            for load in loads:
                load.start()
        pl.semaphore_signal(barrier, inc=1, device_id=peer_at(here, offset), device_id_type=MESH)
    for load in loads:
        load.wait()

    label = lab_ref[...]
    label_high, label_low = label >> 7, label & 127
    slot8 = slot8_ref[...]
    table = jnp.concatenate([slot8 // owned, slot8 % owned], axis=0).astype(F32).astype(BF16)
    high_hit = iota((half, count), 0) == label_high
    owner = jnp.sum(
        jnp.where(high_hit, pick_lanes(slot8_ref[...], label_low), 0), axis=0, keepdims=True
    )
    dest, local_group = owner // owned, owner % owned

    hot_low = onehot(label_low, LANES)
    high_one = jnp.where(high_hit, 1.0, 0.0)
    none = jnp.zeros((half, LANES), F32)
    prior = jnp.concatenate([
        jnp.concatenate([
            high_one[:, other * LANES : (other + 1) * LANES] if other < block else none
            for other in range(blocks)
        ], axis=1)
        for block in range(blocks)
    ], axis=0).astype(BF16)
    tables = dot_nt(prior, hot_low)
    columns = jnp.concatenate(
        [lab16_ref[...], jnp.zeros((LANES - blocks, LANES), I32)], axis=0
    ).astype(F32).T.astype(I32)
    triangle = jnp.where(iota((LANES, LANES), 0) < iota((LANES, LANES), 1), 1.0, 0.0)
    ranks = []
    for block in range(blocks):
        lanes = slice(block * LANES, (block + 1) * LANES)
        column = jnp.broadcast_to(columns[:, block : block + 1], (LANES, LANES))
        within = jnp.where(column == label[:, lanes], triangle, 0.0)
        before = jnp.where(
            high_hit[:, lanes], pick_lanes(tables[block * half : (block + 1) * half], label_low[:, lanes]), 0.0
        )
        within = jnp.sum(within.reshape(LANES // half, half, LANES), axis=0)
        ranks.append(jnp.sum(before + within, axis=0, keepdims=True))
    rank = jnp.concatenate(ranks, axis=1).astype(I32)
    slot = local_group * MOST + rank

    hot_dest[...] = onehot(dest, devices)
    slot_hit = iota((slots, count), 0) == slot
    fields = [mass_ref[...], pos_ref[0:1, :], pos_ref[1:2, :], pos_ref[2:3, :],
              vel_ref[0:1, :], vel_ref[1:2, :], vel_ref[2:3, :]]
    split = [[part.astype(F32) for part in parts_of(field, 3)] for field in fields]
    outgoing = None
    for part in range(3):
        chosen = [jnp.where(slot_hit, split[f][part], 0.0).astype(BF16) for f in range(7)]
        chosen.append(jnp.zeros((slots, count), BF16))
        product = dot_nt(hot_dest[...], jnp.concatenate(chosen, axis=0))
        outgoing = product if outgoing is None else outgoing + product
    out1[...] = outgoing

    slot_row = slot_ref[...]
    mine = jnp.where(iota((LANES, groups), 0) // MOST == slot_row - me * owned, 1.0, 0.0).astype(BF16)
    limits = jnp.minimum(cap_ref[...], CAP)
    limit_parts = jnp.concatenate([limits // 64, limits % 64], axis=0).astype(F32).astype(BF16)
    limit = dot_nt(limit_parts, mine)
    limit = limit[0:1] * 64.0 + limit[1:2]
    away = order_ref[...]
    source = (((mx // 4 + away[0:1]) & 3) * 4 + ((mx + away[1:2]) & 3)) * ny + (
        ((my // 2 + away[2:3]) & 3) * 2 + ((my + away[3:4]) & 1)
    )
    source = jnp.broadcast_to(source.astype(F32), (LANES, LANES))
    lower = jnp.where(source < source.T, 1.0, 0.0).astype(BF16)
    quad = jnp.where(
        iota((LANES, LANES), 0) // MOST == iota((LANES, LANES), 1) // MOST, 1.0, 0.0
    ).astype(BF16)
    quarter = (iota((1, LANES), 1) % MOST).astype(F32)

    pl.semaphore_wait(barrier, devices - 1)
    here = (mx, my)
    places = near_first()
    for offset in far_first():
        back = places.index(tuple((size - step) % size for step, size in zip(offset, (4, 4, 4, 2))))
        px, py = peer_at(here, offset)
        pltpu.make_async_remote_copy(
            src_ref=out1.at[pl.ds(px * ny + py, 1)],
            dst_ref=got1.at[pl.ds(back, 1)],
            send_sem=send1,
            recv_sem=recv1,
            device_id=(px, py),
            device_id_type=MESH,
        ).start()
    own = pl.ds(me, 1)
    pltpu.make_async_copy(out1.at[own], got1.at[pl.ds(0, 1)], recv1).start()
    pltpu.make_async_copy(out1.at[own], spare1.at[own], send1).start()

    lane = iota((1, LANES), 1)
    lane8 = iota((8, LANES), 1)
    offset8 = lane8 - iota((8, LANES), 0)

    def row_of(ref, at):
        return jnp.broadcast_to(ref[at : at + 1, :], (8, LANES))

    def column_of(block, at):
        return jnp.broadcast_to(block[:, at : at + 1], (8, LANES))

    def inverse_of(target, there):
        ax, ay, az = [t - h for t, h in zip(target, there)]
        return lax.rsqrt(ax * ax + ay * ay + az * az + SOFTENING_SQ)

    pltpu.make_async_copy(got1, got1, recv1).wait()
    pltpu.make_async_copy(out1, out1, send1).wait()

    first = got1[:, :LANES]
    is_mass = lane < slots
    valid = is_mass & (first > 0.0)
    earlier = dot(lower, jnp.where(valid, 1.0, 0.0).astype(BF16))
    member_rank = dot(earlier.astype(BF16), quad) + quarter
    keep = valid & (member_rank < limit)
    kept_mass = jnp.where(keep, first, 0.0)
    rows_ref[slots:] = first.T[slots:]
    rows_ref[:slots] = kept_mass.T[:slots]
    kept_total = quad_sum(jnp.sum(jnp.where(keep, 1.0, 0.0), axis=0, keepdims=True))
    mass_sum = quad_sum(jnp.sum(kept_mass, axis=0, keepdims=True))
    second = got1[:, LANES:]
    stats = [mass_sum * (1.0 / CAP)]
    energy = None
    for axis in range(3):
        speed = second if axis == 0 else pltpu.roll(second, LANES - axis * slots, 1)
        bulk = quad_sum(jnp.sum(kept_mass * speed, axis=0, keepdims=True)) / mass_sum
        stats.append(bulk)
        apart = (speed - bulk) * (speed - bulk)
        energy = apart if energy is None else energy + apart
    motion[...] = jnp.where(lane < slots, 0.5 * energy, 0.0)
    rank_or_not = jnp.where(keep, member_rank, -1.0)
    member[...] = jnp.where(
        lane < 3 * slots,
        pltpu.roll(rank_or_not, 2 * slots, 1),
        jnp.broadcast_to(
            jnp.take_along_axis(
                jnp.broadcast_to(kept_total, (8, LANES)), (iota((8, LANES), 1) % owned) * MOST, axis=1
            )[0:1],
            (devices, LANES),
        ),
    )
    spot8 = lane8 % slots
    ones = jnp.ones((2 * LANES, LANES), BF16)

    def conclude(block):
        at = pl.ds(block * 8, 8)
        sums = dot(halves[...], ones)
        pot = jnp.zeros((8, LANES), F32)
        for spot in range(slots):
            pot = jnp.where(spot8 == spot, sums[spot * 8 : spot * 8 + 8], pot)
        both = pot * (-1.0 / CAP) + motion[at, :]
        out2[at, :] = jnp.where(lane8 < 2 * slots, both, member[at, :])

    def pairs_of(block):
        targets = got1[block * 8 : block * 8 + 8, :LANES]
        itself = offset8 == block * 8
        for group in range(owned):
            base = group * MOST
            there = [[row_of(rows_ref, f * slots + base + r) for f in range(4)] for r in range(MOST)]
            totals = []
            for r in range(MOST):
                target = [column_of(targets, f * slots + base + r) for f in range(1, 4)]
                total = None
                for other in range(MOST):
                    value = inverse_of(target, there[other][1:])
                    if r == other:
                        value = jnp.where(itself, 0.0, value)
                    term = value * there[other][0]
                    total = term if total is None else total + term
                totals.append(total)
            for pair in range(0, MOST, 2):
                high, low = parts_of(jnp.concatenate(totals[pair : pair + 2], axis=0), 2)
                lines = pl.ds((group * MOST + pair) * 8, 16)
                halves[lines, :LANES] = high
                halves[lines, LANES:] = low

    def send_block(block):
        for place in range(block * 8 + 7, block * 8 - 1, -1):
            if place:
                pltpu.make_async_remote_copy(
                    src_ref=out2.at[pl.ds(place, 1)],
                    dst_ref=got2.at[own],
                    send_sem=send2,
                    recv_sem=recv2,
                    device_id=peer_at(here, places[place]),
                    device_id_type=MESH,
                ).start()

    last = devices // 8 - 1
    gone = []
    for block in range(last, -1, -1):
        if block < last - 1:
            conclude(block + 1)
            gone.append(block + 1)
        pairs_of(block)
        if block == last:
            conclude(block)
            gone.append(block)
        if block >= last - 2 or block <= 5 or block % 2 == 0:
            for ready in gone:
                send_block(ready)
            gone = []
    conclude(0)
    send_block(0)
    pltpu.make_async_copy(out2.at[pl.ds(0, 1)], got2.at[own], recv2).start()
    pltpu.make_async_copy(out2.at[pl.ds(0, 1)], spare2.at[own], send2).start()
    pick = iota((LANES, owned), 0) == iota((LANES, owned), 1) * MOST
    stat_rows = jnp.concatenate(stats + [jnp.zeros((LANES - 4, LANES), F32)], axis=0).T
    for number in range(4):
        cat_ref[number : number + 1, :] = jnp.sum(
            jnp.where(pick, stat_rows[:, number : number + 1], 0.0), axis=0, keepdims=True
        )
    upper = jnp.where(iota((LANES, LANES), 0) < iota((LANES, LANES), 1), 1.0, 0.0).astype(BF16)
    pltpu.make_async_copy(out2, out2, send2).wait()
    pltpu.make_async_copy(got2, got2, recv2).wait()
    answer = got2[...].T
    kept_of = pick_lanes(answer[3 * slots : 3 * slots + owned], slot_row // owned)
    kept_row = jnp.sum(
        jnp.where(iota((owned, groups), 0) == slot_row % owned, kept_of, 0.0), axis=0, keepdims=True
    )
    kept8 = jnp.concatenate(
        [kept_row[:, i * LANES : (i + 1) * LANES] for i in range(half)], axis=0
    )
    kept_parts = parts_of(kept8, 2)
    start8 = dot(kept_parts[0], upper) + dot(kept_parts[1], upper)
    ahead = jnp.broadcast_to(jnp.sum(kept8, axis=1, keepdims=True), (half, LANES))
    row8 = iota((half, LANES), 0)
    ahead = jnp.where(row8 >= 1, pltpu.roll(ahead, 1, 0), 0.0)
    for step in (1, 2, 4):
        ahead = ahead + jnp.where(row8 >= step, pltpu.roll(ahead, step, 0), 0.0)
    start8 = start8 + ahead
    start = jnp.sum(jnp.where(high_hit, pick_lanes(start8, label_low), 0.0), axis=0, keepdims=True)
    first_pieces = [dot(piece, hot_dest[...]) for piece in parts_of(answer[:slots], 3)]
    found = [first_pieces[0] + first_pieces[1] + first_pieces[2]]
    found += [pick_lanes(answer[v * slots : (v + 1) * slots], dest) for v in (1, 2)]
    chosen = [
        jnp.sum(jnp.where(slot_hit, value, 0.0), axis=0, keepdims=True) for value in found
    ]
    kept = chosen[2] >= 0.0
    index_ref[...] = jnp.where(kept, start + chosen[2], -1.0).astype(I32)
    pot_ref[...] = jnp.where(kept, chosen[1], 0.0)
    bind_ref[...] = jnp.where(kept, chosen[0], 0.0)


def finish(*refs):
    half = len(refs) // 2
    for source, result in zip(refs[:half], refs[half:]):
        result[...] = source[...]


def shards(sizes, positions, velocities, masses, labels, owner_slot, group_cap):
    nx, ny = sizes
    count = masses.shape[0]
    groups = owner_slot.shape[0]
    owned = groups // (nx * ny)
    slots = owned * MOST
    vmem = pl.BlockSpec(memory_space=pltpu.VMEM)
    devices = nx * ny
    wide = lambda width: pltpu.VMEM((devices, width), F32)
    label_row = labels.reshape(1, count)
    slot_row = owner_slot.reshape(1, groups)
    row = lambda dtype: jax.ShapeDtypeStruct((1, count), dtype)
    results = (row(I32), row(F32), row(F32), jax.ShapeDtypeStruct((4, owned), F32))
    inputs = (
        label_row, labels.reshape(count // LANES, LANES), positions, velocities,
        masses.reshape(1, count), owner_slot.reshape(groups // LANES, LANES),
        slot_row, group_cap.reshape(1, groups),
        jnp.array(near_first(), I32).T,
    )
    found = pl.pallas_call(
        functools.partial(kernel, sizes),
        out_shape=results,
        in_specs=[pl.BlockSpec(memory_space=pltpu.HBM)] * 9,
        out_specs=(vmem,) * 4,
        scratch_shapes=[
            *[pltpu.VMEM(array.shape, array.dtype) for array in inputs],
            *[wide(2 * LANES)] * 3,
            *[wide(LANES)] * 3,
            pltpu.VMEM((devices, count), BF16),
            wide(LANES),
            *[wide(LANES)] * 2,
            pltpu.VMEM((slots * 8, 2 * LANES), BF16),
            pltpu.SemaphoreType.DMA((9,)),
            *[pltpu.SemaphoreType.DMA] * 4,
        ],
        compiler_params=pltpu.CompilerParams(
            collective_id=0, has_side_effects=True, vmem_limit_bytes=24 * 2**20
        ),
        name="unbind",
    )(*[pltpu.with_memory_space_constraint(array, pltpu.HBM) for array in inputs])
    index, pot, bind, catalog = pl.pallas_call(
        finish,
        out_shape=results,
        in_specs=[vmem] * 4,
        out_specs=(vmem,) * 4,
        compiler_params=pltpu.CompilerParams(vmem_limit_bytes=2**20),
        name="finish",
    )(*found)
    return (index.reshape(count), pot.reshape(count), bind.reshape(count), catalog)


def solution(mesh):
    sizes = (mesh.shape["gx"], mesh.shape["gy"])
    return jax.shard_map(
        functools.partial(shards, sizes),
        mesh=mesh,
        in_specs=(
            P(None, ("gx", "gy")),
            P(None, ("gx", "gy")),
            P(("gx", "gy")),
            P(("gx", "gy"), None),
            P(),
            P(),
        ),
        out_specs=(P(("gx", "gy")), P(("gx", "gy")), P(("gx", "gy")), P(None, ("gx", "gy"))),
        check_vma=False,
    )
```
